128 devices in a mesh: row: 8 (over y, core), col: 16 (over z, x).
Axes of the slice: x: 4, y: 4, z: 4, core: 2. Of those that a mesh axis runs over, the one named last changes fastest.
Arguments:
- shot_boxes: int32 [4, 8, 16384], P(None, 'row', 'col'), may hold values from 0 to 512, as said below
- block_counts: int32 [8, 16], P('row'), may hold values from 1 to 8, 64 in all within a row
- tail_shots: int32 [8, 16], P('row'), may hold values from 1 to 128
- doses: float32 [8, 16384], P('row', 'col'), may hold values from 0.5 to 1.5
- pixel_gain: float32 [4096, 8192], P('row', 'col'), may hold values from 0.6 to 1.6
Outputs:
- corrected: float32 [8, 16384], P('row', 'col')
- exposure: float32 [8, 16384], P('row', 'col')
The draws below stay inside these ranges and needn't reach their ends.
Inputs may be any that keep to these rules, and one draw needn't show every extreme that they name: `shot_boxes`: every shot has 8 <= x1 - x0 <= 64 and 8 <= y1 - y0 <= 64, inside its tile of 512 pixels. `block_counts`: in every tile row the block counts sum to exactly 64, and some tile of the row has 8.
All inputs are finite; a program needn't handle non-finite values.
Results may differ from the reference program's by a relative error of at most 0.0003.
Values sent between devices are 32-bit elements; how exact they have to be, the bound alone decides.
No kernel may reach another device: no remote copies, remote signals or barrier semaphores. Data moves between devices by JAX's collectives and lax.ppermute only.
A program may use at most 64 MiB of HBM per device.

```python
import math
import jax
import jax.numpy as jnp
import numpy as np
from jax import lax

TILE = 512
CG = 128
BLK = 128
MAXB = 8
RCAP = 4
ITERS = 3
CELL = 4
BETA = 16
REACH = 32
WMAX = 64
SLOTS = 1024
NTR = 8
NTC = 16
N_COL = 16


def draw_shot_boxes(key, part):
    keys = jax.random.split(jax.random.fold_in(key, 17), 4)
    layout = (NTR, NTC * SLOTS)
    left_side = jax.random.randint(keys[0], layout, 0, TILE - WMAX + 1)
    top_side = jax.random.randint(keys[1], layout, 0, TILE - WMAX + 1)
    wide_side = jax.random.randint(keys[2], layout, 8, WMAX + 1)
    tall_side = jax.random.randint(keys[3], layout, 8, WMAX + 1)
    return jnp.stack([left_side, top_side, left_side + wide_side, top_side + tall_side]).astype(jnp.int32)


def plant(result, own_key, low, largest):
    extent = result.shape
    spot = [jax.random.randint(jax.random.fold_in(own_key, axis), (), 0, extent[axis]) for axis in range(len(extent))]
    result = result.at[tuple(spot)].set(low)
    longest = extent.index(max(extent))
    spot[longest] = (spot[longest] + 1) % extent[longest]
    return result.at[tuple(spot)].set(largest)


def steps_of(rng, dims, cuts, least, high):
    def one(dim, parts):
        steps = jax.random.uniform(jax.random.fold_in(jax.random.fold_in(rng, 6), dim), (parts,), jnp.float32, least / len(cuts), high / len(cuts))
        return jnp.repeat(jnp.exp(steps), dims[dim] // parts).reshape((-1,) + (1,) * (len(dims) - dim - 1))

    level = one(*cuts[0])
    for cut in cuts[1:]:
        level = level * one(*cut)
    return level


def profile(count, total, most, slope):
    portions = [(1 << 20) // math.isqrt(grade ** slope) + 1 for grade in range(2, count + 1)]
    rest, counts = total - most - (count - 1), [1] * (count - 1)
    while rest > 0:
        candidates = [i for i in range(count - 1) if counts[i] < most]
        whole, remaining = sum([portions[i] for i in candidates]), rest
        for i in candidates:
            addition = min(most - counts[i], max(1, remaining * portions[i] // whole), rest)
            counts[i] = counts[i] + addition
            rest = rest - addition
    return np.array([most] + counts)


def uneven_parts(key, number_of, total, limit, lean):
    if number_of == 2:
        one = jax.random.randint(key, (), max(1, total - limit), min(limit, total - 1) + 1)
        return jnp.stack([one, total - one])
    tallies = jnp.asarray(profile(number_of, total, limit, lean), jnp.int32)
    couples = (number_of - 1) // 2
    source_of, receiver = tallies[1:1 + 2 * couples:2], tallies[2:2 + 2 * couples:2]
    room = jnp.minimum(source_of - 1, limit - receiver)
    shifted = jax.random.randint(jax.random.fold_in(key, 1), (couples,), 0, 1 << 20) % (room + 1)
    tallies = tallies.at[1:1 + 2 * couples:2].set(source_of - shifted).at[2:2 + 2 * couples:2].set(receiver + shifted)
    return tallies[jax.random.permutation(jax.random.fold_in(key, 2), number_of)]


def setup_inputs(seed: int = 0) -> dict:
    streams_of = jax.random.split(jax.random.key(seed), 6)
    return {
        "shot_boxes": draw_shot_boxes(jax.random.fold_in(streams_of[5], 71), 0),
        "block_counts": jax.vmap(lambda own: uneven_parts(own, NTC, RCAP * N_COL, MAXB, 2))(jax.random.split(streams_of[1], NTR)).reshape((NTR, NTC)).astype(jnp.int32),
        "tail_shots": plant(jax.random.randint(streams_of[2], (NTR, NTC), 1, BLK + 1), jax.random.fold_in(streams_of[2], 1), 1, BLK).astype(jnp.int32),
        "doses": jnp.clip(0.5 + 1.0 * jax.random.uniform(streams_of[3], (NTR, NTC * SLOTS), jnp.float32) ** steps_of(streams_of[3], (NTR, NTC * SLOTS), ((0, 8), (1, 16)), -0.2, 0.2), 0.5, 1.5),
        "pixel_gain": jnp.clip(jnp.exp(math.log(1.6) - 0.98082923 * jax.random.uniform(streams_of[4], (NTR * TILE, NTC * TILE), jnp.float32) ** steps_of(streams_of[4], (NTR * TILE, NTC * TILE), ((0, 8), (1, 16)), -0.2, 0.2)), 0.6, 1.6),
    }


FORWARD_RANGE = 4.0
BACK_RATIO = 0.75
TARGET_LEVEL = 1.0
EXACT_MODE = lax.Precision.HIGHEST

def edge_term(doubled, low_edge, high_edge):
    middle = doubled.astype(jnp.float32)[None, :] * 0.5
    low_side = low_edge.astype(jnp.float32)[:, None]
    high_side = high_edge.astype(jnp.float32)[:, None]
    return 0.5 * (jax.scipy.special.erf((middle - low_side) / FORWARD_RANGE) - jax.scipy.special.erf((middle - high_side) / FORWARD_RANGE))

def pair_kernel(sources, centres):
    return edge_term(centres[0], sources[0], sources[2]) * edge_term(centres[1], sources[1], sources[3])

def intersection(low_edge, high_edge):
    cell_edges = jnp.arange(CG, dtype=jnp.int32) * CELL
    covered = jnp.minimum(high_edge[:, None], cell_edges[None, :] + CELL) - jnp.maximum(low_edge[:, None], cell_edges[None, :])
    return jnp.maximum(covered, 0).astype(jnp.float32) / CELL

def spread(distance):
    scaled = distance.astype(jnp.float32) / BETA
    inside = jnp.abs(distance) <= REACH
    return jnp.where(inside, jnp.exp(-scaled * scaled) / (math.sqrt(math.pi) * BETA), 0.0)

def tile_kernel(packed):
    return pair_kernel(packed[0], packed[1])

def reference(shot_boxes, block_counts, tail_shots, doses, pixel_gain):
    tile_count = NTR * NTC
    tiles = jnp.transpose(shot_boxes.reshape(4, NTR, NTC, SLOTS), (1, 2, 0, 3)).reshape(tile_count, 4, SLOTS)
    totals = ((block_counts - 1) * BLK + tail_shots).reshape(tile_count)
    is_live = jnp.arange(SLOTS, dtype=jnp.int32)[None, :] < totals[:, None]
    shot_dose = jnp.where(is_live, doses.reshape(tile_count, SLOTS), 0.0)
    centres = jnp.stack([tiles[:, 0] + tiles[:, 2], tiles[:, 1] + tiles[:, 3]], axis=1)
    kernels = lax.map(tile_kernel, (tiles, centres))
    across = jax.vmap(intersection)(tiles[:, 0], tiles[:, 2])
    downward = jax.vmap(intersection)(tiles[:, 1], tiles[:, 3])
    cell_ids = centres[:, 1] // (2 * CELL) * CG + centres[:, 0] // (2 * CELL)
    pixel_ids = (centres[:, 1] // 2 * TILE + centres[:, 0] // 2).astype(jnp.int32)
    gain_tiles = jnp.transpose(pixel_gain.reshape(NTR, TILE, NTC, TILE), (0, 2, 1, 3)).reshape(tile_count, TILE * TILE)
    sensitive = jnp.take_along_axis(gain_tiles, pixel_ids, axis=1)
    row_cells = jnp.arange(NTR * CG, dtype=jnp.int32)
    col_cells = jnp.arange(NTC * CG, dtype=jnp.int32)
    row_blur = spread(row_cells[:, None] - row_cells[None, :])
    col_blur = spread(col_cells[:, None] - col_cells[None, :])
    exposure = jnp.zeros_like(shot_dose)
    for sweep in range(ITERS):
        forward = jnp.einsum('nj,nji->ni', shot_dose, kernels, precision=EXACT_MODE)
        coarse = jnp.einsum('nsy,nsx->nyx', downward, shot_dose[:, :, None] * across, precision=EXACT_MODE)
        window = jnp.transpose(coarse.reshape(NTR, NTC, CG, CG), (0, 2, 1, 3)).reshape(NTR * CG, NTC * CG)
        blurred = jnp.dot(row_blur, window, precision=EXACT_MODE)
        background = jnp.dot(blurred, col_blur, precision=EXACT_MODE)
        tile_maps = jnp.transpose(background.reshape(NTR, CG, NTC, CG), (0, 2, 1, 3)).reshape(tile_count, CG * CG)
        sampled = jnp.take_along_axis(tile_maps, cell_ids, axis=1)
        exposure = sensitive * (forward + BACK_RATIO * sampled) / (1.0 + BACK_RATIO)
        shot_dose = jnp.where(is_live, shot_dose * TARGET_LEVEL / jnp.where(is_live, exposure, 1.0), 0.0)
    corrected = shot_dose.reshape(NTR, NTC * SLOTS)
    final_exposure = jnp.where(is_live, exposure, 0.0).reshape(NTR, NTC * SLOTS)
    return (corrected, final_exposure)
```

```python
import functools
import math

import jax
import jax.numpy as jnp
from jax import lax
from jax.experimental import pallas as pl
from jax.experimental.pallas import tpu as pltpu
from jax.sharding import PartitionSpec as P

TILE = 512
CG = 128
BLK = 128
ITERS = 3
CELL = 4
BETA = 16
REACH = 32
SLOTS = 1024
NTR = 8
NTC = 16
FORWARD_RANGE = 4.0
BACK_RATIO = 0.75
TARGET_LEVEL = 1.0
F32 = jnp.float32
BF16 = jnp.bfloat16
AXES = ("row", "col")
NT = (((1,), (1,)), ((), ()))


def pairings():
    def number(r, c):
        return r * NTC + c

    def table(partner):
        return [(number(r, c), number(*partner(r, c))) for r in range(NTR) for c in range(NTC)]

    def odd(i):
        return ((i - 1) ^ 1) + 1

    row_even = table(lambda r, c: (r ^ 1, c))
    row_odd = table(lambda r, c: (r, c ^ 1) if r in (0, NTR - 1) else (odd(r), c))
    col_even = table(lambda r, c: (r, c ^ 1))
    col_odd = table(lambda r, c: (r ^ 1, c) if c in (0, NTC - 1) else (r, odd(c)))
    return row_even, row_odd, col_even, col_odd


def two_parts(value):
    high = value.astype(BF16)
    low = (value - high.astype(F32)).astype(BF16)
    return high, low


def stacked_dot(value, other, dims):
    rows = value.shape[0]
    parts = jnp.concatenate(two_parts(value), axis=0)
    both = lax.dot_general(parts, other, dims, preferred_element_type=F32)
    return both[:rows] + both[rows:]


def weighted(value, high, low):
    rows = value.shape[0]
    first, second = two_parts(value)
    both = jnp.dot(jnp.concatenate([first, second], axis=0), high, preferred_element_type=F32)
    return both[:rows] + both[rows:] + jnp.dot(first, low, preferred_element_type=F32)


def overlap(low_edge, high_edge, cells):
    begin = cells * CELL
    covered = jnp.minimum(high_edge, begin + CELL) - jnp.maximum(low_edge, begin)
    return jnp.maximum(covered, 0).astype(F32) * (1.0 / CELL)


def spread(distance):
    scaled = distance.astype(F32) / BETA
    inside = jnp.abs(distance) <= REACH
    return jnp.where(inside, jnp.exp(-scaled * scaled) / (math.sqrt(math.pi) * BETA), 0.0)


def iota(shape, axis):
    return lax.broadcasted_iota(jnp.int32, shape, axis)


def is_even(axis):
    return lax.rem(lax.axis_index(axis), 2) == 0


def row_strips(dose, px_t, py_edges, send_even, send_odd):
    edges = stacked_dot(py_edges * dose, px_t, NT)
    top, bottom = edges[:REACH], edges[REACH:]
    even = is_even("row")
    send_even[...] = jnp.where(even, bottom, top)
    send_odd[...] = jnp.where(even, top, bottom)


def start_kernel(boxes, counts, tails, doses, dose_out, send_even, send_odd):
    col = lax.axis_index("col")
    totals = (counts[...] - 1) * BLK + tails[...]
    total = jnp.sum(jnp.where(iota((1, NTC), 1) == col, totals, 0), axis=1, keepdims=True)
    live = iota((1, SLOTS), 1) < total
    dose = jnp.where(live, doses[...], 0.0)
    dose_out[...] = dose
    px_t = overlap(boxes[0], boxes[2], iota((CG, SLOTS), 0)).astype(BF16)
    edge_cells = iota((2 * REACH, SLOTS), 0)
    edge_cells = jnp.where(edge_cells < REACH, edge_cells, edge_cells + (CG - 2 * REACH))
    py_edges = overlap(boxes[1], boxes[3], edge_cells)
    row_strips(dose, px_t, py_edges, send_even, send_odd)


def sens_kernel(boxes, gain, px_out, py_out, sens_out):
    px_out[...] = overlap(boxes[0], boxes[2], iota((CG, SLOTS), 0)).astype(BF16)
    py_out[...] = overlap(boxes[1], boxes[3], iota((CG, SLOTS), 0)).astype(BF16)
    pixel_x = (boxes[0] + boxes[2]) // 2
    pixel_y = (boxes[1] + boxes[3]) // 2
    pixels = iota((TILE, SLOTS), 0)
    chosen_x = jnp.where(pixels == pixel_x, 1.0, 0.0).astype(BF16)
    picked = stacked_dot(gain[...], chosen_x, (((1,), (0,)), ((), ())))
    sens_out[...] = jnp.sum(jnp.where(pixels == pixel_y, picked, 0.0), axis=0, keepdims=True)


def setup_kernel(boxes, wy_high, wy_low, wx_out, pairs):
    cell_x = (boxes[0] + boxes[2]) // (2 * CELL)
    cell_y = (boxes[1] + boxes[3]) // (2 * CELL)
    y = iota((2 * CG, SLOTS), 0)
    place = jnp.where(y < CG, y, jnp.where(y < CG + REACH, y - (CG + REACH), y - REACH))
    weight = jnp.where(y < CG + 2 * REACH, spread(cell_y - place), 0.0)
    wy_high[...], wy_low[...] = two_parts(weight)
    x = iota((CG + 2 * REACH, SLOTS), 0)
    place = jnp.where(x < CG, x, jnp.where(x < CG + REACH, x - (CG + REACH), x - REACH))
    wx_out[...] = spread(cell_x - place)
    inverse = 1.0 / FORWARD_RANGE
    box = [boxes[k].astype(F32) for k in range(4)]
    centre_x = (box[0] + box[2]) * (0.5 * inverse)
    centre_y = (box[1] + box[3]) * (0.5 * inverse)
    columns = jnp.concatenate([b * inverse for b in box] + [jnp.zeros((4, SLOTS), F32)], axis=0)
    step = 128
    for first in range(0, SLOTS, step):
        side = jnp.transpose(columns[:, first : first + step])
        along_x = lax.erf(centre_x - side[:, 0:1]) - lax.erf(centre_x - side[:, 2:3])
        along_y = lax.erf(centre_y - side[:, 1:2]) - lax.erf(centre_y - side[:, 3:4])
        pairs[first : first + step, :] = (0.25 * along_x) * along_y


def forward_kernel(dose_in, pairs, forward):
    dose = dose_in[...]
    folded = jnp.concatenate([dose[:, k * 128 : (k + 1) * 128] for k in range(8)], axis=0)
    columns = jnp.transpose(folded)
    total = jnp.zeros((8, SLOTS), F32)
    for k in range(8):
        part = columns[:, k : k + 1] * pairs[k * 128 : (k + 1) * 128, :]
        total += jnp.sum(part.reshape(16, 8, SLOTS), axis=0)
    forward[...] = jnp.sum(total, axis=0, keepdims=True)


def coarse_kernel(dose_in, px, py, coarse_t):
    coarse_t[...] = stacked_dot(px[...].astype(F32) * dose_in[...], py[...], NT)


def middle_kernel(got_even, got_odd, coarse_t, tall_t, send_even, send_odd):
    row = lax.axis_index("row")
    even = lax.rem(row, 2) == 0
    from_even, from_odd = got_even[...], got_odd[...]
    above = jnp.where(even, from_odd, from_even)
    below = jnp.where(even, from_even, from_odd)
    above = jnp.where(row == 0, 0.0, above)
    below = jnp.where(row == NTR - 1, 0.0, below)
    outer = jnp.concatenate([above, below, jnp.zeros((CG - 2 * REACH, CG), F32)], axis=0)
    tall = jnp.concatenate([coarse_t[...], jnp.transpose(outer)], axis=1)
    tall_t[...] = tall
    even = is_even("col")
    left, right = tall[:REACH], tall[CG - REACH :]
    send_even[...] = jnp.where(even, right, left)
    send_odd[...] = jnp.where(even, left, right)


def inner_kernel(tall_t, wy_high, wy_low, wx, inner):
    across = weighted(tall_t[...], wy_high[...], wy_low[...])
    inner[...] = jnp.sum(across * wx[:CG, :], axis=0, keepdims=True)


def new_dose(got_even, got_odd, forward, inner, sens, dose_in, wy_high, wy_low, wx):
    col = lax.axis_index("col")
    even = lax.rem(col, 2) == 0
    from_even, from_odd = got_even[...], got_odd[...]
    left = jnp.where(even, from_odd, from_even)
    right = jnp.where(even, from_even, from_odd)
    left = jnp.where(col == 0, 0.0, left)
    right = jnp.where(col == NTC - 1, 0.0, right)
    across = weighted(jnp.concatenate([left, right], axis=0), wy_high[...], wy_low[...])
    background = inner[...] + jnp.sum(across * wx[CG:, :], axis=0, keepdims=True)
    exposure = sens[...] * (forward[...] + BACK_RATIO * background) / (1.0 + BACK_RATIO)
    dose = dose_in[...]
    live = dose > 0.0
    return jnp.where(live, dose * TARGET_LEVEL / jnp.where(live, exposure, 1.0), 0.0), jnp.where(live, exposure, 0.0)


def update_kernel(got_even, got_odd, forward, inner, sens, dose_in, wy_high, wy_low, wx, px, py, dose_out, send_even, send_odd):
    dose, _ = new_dose(got_even, got_odd, forward, inner, sens, dose_in, wy_high, wy_low, wx)
    dose_out[...] = dose
    py_edges = jnp.concatenate([py[:REACH, :], py[CG - REACH :, :]], axis=0).astype(F32)
    row_strips(dose, px[...], py_edges, send_even, send_odd)


def final_kernel(got_even, got_odd, forward, inner, sens, dose_in, wy_high, wy_low, wx, dose_out, exposure_out):
    dose_out[...], exposure_out[...] = new_dose(got_even, got_odd, forward, inner, sens, dose_in, wy_high, wy_low, wx)


def shape(*dims, dtype=F32):
    return jax.ShapeDtypeStruct(dims, dtype)


def call(kernel, outs, name, vmem=16, flops=0, moved=0):
    return pl.pallas_call(
        kernel,
        out_shape=outs,
        name=name,
        compiler_params=pltpu.CompilerParams(vmem_limit_bytes=vmem << 20),
        cost_estimate=pl.CostEstimate(flops=flops, bytes_accessed=moved, transcendentals=0),
    )


def body(shot_boxes, block_counts, tail_shots, doses, pixel_gain):
    row_even, row_odd, col_even, col_odd = pairings()
    row = shape(1, SLOTS)
    strip = shape(REACH, CG)
    wide = shape(REACH, 2 * CG)
    dose, strip_even, strip_odd = call(start_kernel, (row, strip, strip), "start")(shot_boxes, block_counts, tail_shots, doses)
    for sweep in range(ITERS):
        got_even = lax.ppermute(strip_even, AXES, row_even)
        got_odd = lax.ppermute(strip_odd, AXES, row_odd)
        if sweep == 0:
            px, py, sens = call(sens_kernel, (shape(CG, SLOTS, dtype=BF16), shape(CG, SLOTS, dtype=BF16), row), "sens")(shot_boxes, pixel_gain)
        coarse_t = call(coarse_kernel, shape(CG, CG), "coarse")(dose, px, py)
        tall_t, wide_even, wide_odd = call(middle_kernel, (shape(CG, 2 * CG), wide, wide), "middle")(got_even, got_odd, coarse_t)
        far_even = lax.ppermute(wide_even, AXES, col_even)
        far_odd = lax.ppermute(wide_odd, AXES, col_odd)
        if sweep == 0:
            wy_high, wy_low, wx, pairs = call(
                setup_kernel,
                (shape(2 * CG, SLOTS, dtype=BF16), shape(2 * CG, SLOTS, dtype=BF16), shape(CG + 2 * REACH, SLOTS), shape(SLOTS, SLOTS)),
                "setup",
            )(shot_boxes)
        forward = call(forward_kernel, row, "forward")(dose, pairs)
        inner = call(inner_kernel, row, "inner")(tall_t, wy_high, wy_low, wx)
        common = (far_even, far_odd, forward, inner, sens, dose, wy_high, wy_low, wx)
        if sweep < ITERS - 1:
            dose, strip_even, strip_odd = call(update_kernel, (row, strip, strip), "update")(*common, px, py)
    return call(final_kernel, (row, row), "final")(*common)


def solution(mesh):
    placed = (P(None, "row", "col"), P("row", None), P("row", None), P("row", "col"), P("row", "col"))
    return jax.shard_map(body, mesh=mesh, in_specs=placed, out_specs=(P("row", "col"), P("row", "col")), check_vma=False)
```

```python
import math

import jax
import jax.numpy as jnp
from jax import lax
from jax.experimental import pallas as pl
from jax.experimental.pallas import tpu as pltpu
from jax.sharding import PartitionSpec as P


TILE = 512
CG = 128
BLK = 128
ITERS = 3
CELL = 4
BETA = 16
REACH = 32
SLOTS = 1024
NTR = 8
NTC = 16
FORWARD_RANGE = 4.0
BACK_RATIO = 0.75
TARGET_LEVEL = 1.0
F32 = jnp.float32
BF16 = jnp.bfloat16
AXES = ("row", "col")
NT = (((1,), (1,)), ((), ()))
MAXB = 8
EARLY = 5 * BLK


def pairings():
    def number(r, c):
        return r * NTC + c

    def table(partner):
        return [(number(r, c), number(*partner(r, c))) for r in range(NTR) for c in range(NTC)]

    def odd(i):
        return ((i - 1) ^ 1) + 1

    row_even = table(lambda r, c: (r ^ 1, c))
    row_odd = table(lambda r, c: (r, c ^ 1) if r in (0, NTR - 1) else (odd(r), c))
    col_even = table(lambda r, c: (r, c ^ 1))
    col_odd = table(lambda r, c: (r ^ 1, c) if c in (0, NTC - 1) else (r, odd(c)))
    return row_even, row_odd, col_even, col_odd


def two_parts(value):
    high = value.astype(BF16)
    low = (value - high.astype(F32)).astype(BF16)
    return high, low


def stacked_dot(value, other, dims):
    rows = value.shape[0]
    parts = jnp.concatenate(two_parts(value), axis=0)
    both = lax.dot_general(parts, other, dims, preferred_element_type=F32)
    return both[:rows] + both[rows:]


def weighted(value, high, low):
    rows = value.shape[0]
    first, second = two_parts(value)
    both = jnp.dot(jnp.concatenate([first, second], axis=0), high, preferred_element_type=F32)
    return both[:rows] + both[rows:] + jnp.dot(first, low, preferred_element_type=F32)


def overlap(low_edge, high_edge, cells):
    begin = cells * CELL
    covered = jnp.minimum(high_edge, begin + CELL) - jnp.maximum(low_edge, begin)
    return jnp.maximum(covered, 0).astype(F32) * (1.0 / CELL)


def spread(distance):
    scaled = distance.astype(F32) / BETA
    inside = jnp.abs(distance) <= REACH
    return jnp.where(inside, jnp.exp(-scaled * scaled) / (math.sqrt(math.pi) * BETA), 0.0)


def iota(shape, axis):
    return lax.broadcasted_iota(jnp.int32, shape, axis)


def is_even(axis):
    return lax.rem(lax.axis_index(axis), 2) == 0


def row_strips(dose, px_t, py_edges, send_even, send_odd):
    edges = stacked_dot(py_edges * dose, px_t, NT)
    top, bottom = edges[:REACH], edges[REACH:]
    even = is_even("row")
    send_even[...] = jnp.where(even, bottom, top)
    send_odd[...] = jnp.where(even, top, bottom)


def start_kernel(boxes_in, counts_in, tails_in, doses_in, boxes, dose_out, send_even, send_odd, counts, tails, doses, arrived):
    copies = [
        pltpu.make_async_copy(source, target, arrived.at[k])
        for k, (source, target) in enumerate(((boxes_in, boxes), (counts_in, counts), (tails_in, tails), (doses_in, doses)))
    ]
    for copy in copies:
        copy.start()
    for copy in copies:
        copy.wait()
    col = lax.axis_index("col")
    totals = (counts[...] - 1) * BLK + tails[...]
    total = jnp.sum(jnp.where(iota((1, NTC), 1) == col, totals, 0), axis=1, keepdims=True)
    live = iota((1, SLOTS), 1) < total
    dose = jnp.where(live, doses[...], 0.0)
    dose_out[...] = dose
    px_t = overlap(boxes[0], boxes[2], iota((CG, SLOTS), 0)).astype(BF16)
    edge_cells = iota((2 * REACH, SLOTS), 0)
    edge_cells = jnp.where(edge_cells < REACH, edge_cells, edge_cells + (CG - 2 * REACH))
    py_edges = overlap(boxes[1], boxes[3], edge_cells)
    row_strips(dose, px_t, py_edges, send_even, send_odd)


def build_pairs(boxes, pairs, first_shot):
    inverse = 1.0 / FORWARD_RANGE
    box = [boxes[k].astype(F32) for k in range(4)]
    centre_x = (box[0] + box[2]) * (0.5 * inverse)
    centre_y = (box[1] + box[3]) * (0.5 * inverse)
    columns = jnp.concatenate([b * inverse for b in box] + [jnp.zeros((4, SLOTS), F32)], axis=0)
    for at in range(0, pairs.shape[0], BLK):
        side = jnp.transpose(columns[:, first_shot + at : first_shot + at + BLK])
        along_x = lax.erf(centre_x - side[:, 0:1]) - lax.erf(centre_x - side[:, 2:3])
        along_y = lax.erf(centre_y - side[:, 1:2]) - lax.erf(centre_y - side[:, 3:4])
        pairs[at : at + BLK, :] = (0.25 * along_x) * along_y


def early_kernel(boxes, dose_in, gain_in, px_out, py_out, coarse_t, pairs, gain, arrived):
    copy = pltpu.make_async_copy(gain_in, gain, arrived)
    copy.start()
    px = overlap(boxes[0], boxes[2], iota((CG, SLOTS), 0))
    py = overlap(boxes[1], boxes[3], iota((CG, SLOTS), 0)).astype(BF16)
    px_out[...] = px.astype(BF16)
    py_out[...] = py
    coarse_t[...] = stacked_dot(px * dose_in[...], py, NT)
    build_pairs(boxes, pairs, 0)
    copy.wait()


def late_kernel(boxes, gain, wy_high, wy_low, wx_out, pairs, sens_out):
    cell_x = (boxes[0] + boxes[2]) // (2 * CELL)
    cell_y = (boxes[1] + boxes[3]) // (2 * CELL)
    y = iota((2 * CG, SLOTS), 0)
    place = jnp.where(y < CG, y, jnp.where(y < CG + REACH, y - (CG + REACH), y - REACH))
    weight = jnp.where(y < CG + 2 * REACH, spread(cell_y - place), 0.0)
    wy_high[...], wy_low[...] = two_parts(weight)
    x = iota((CG + 2 * REACH, SLOTS), 0)
    place = jnp.where(x < CG, x, jnp.where(x < CG + REACH, x - (CG + REACH), x - REACH))
    wx_out[...] = spread(cell_x - place)
    pixel_x = (boxes[0] + boxes[2]) // 2
    pixel_y = (boxes[1] + boxes[3]) // 2
    pixels = iota((TILE, SLOTS), 0)
    chosen_x = jnp.where(pixels == pixel_x, 1.0, 0.0).astype(BF16)
    picked = stacked_dot(gain[...], chosen_x, (((1,), (0,)), ((), ())))
    sens_out[...] = jnp.sum(jnp.where(pixels == pixel_y, picked, 0.0), axis=0, keepdims=True)
    build_pairs(boxes, pairs, EARLY)


def forward_kernel(dose_in, early_pairs, late_pairs, forward):
    dose = dose_in[...]
    folded = jnp.concatenate([dose[:, k * BLK : (k + 1) * BLK] for k in range(MAXB)], axis=0)
    columns = jnp.transpose(folded)
    total = jnp.zeros((8, SLOTS), F32)
    for k in range(MAXB):
        at = k * BLK
        pairs = early_pairs[at : at + BLK, :] if at < EARLY else late_pairs[at - EARLY : at - EARLY + BLK, :]
        total += jnp.sum((columns[:, k : k + 1] * pairs).reshape(BLK // 8, 8, SLOTS), axis=0)
    forward[...] = jnp.sum(total, axis=0, keepdims=True)


def coarse_kernel(dose_in, px, py, coarse_t):
    coarse_t[...] = stacked_dot(px[...].astype(F32) * dose_in[...], py[...], NT)


def middle_kernel(got_even, got_odd, coarse_t, tall_t, send_even, send_odd):
    row = lax.axis_index("row")
    even = lax.rem(row, 2) == 0
    from_even, from_odd = got_even[...], got_odd[...]
    above = jnp.where(even, from_odd, from_even)
    below = jnp.where(even, from_even, from_odd)
    above = jnp.where(row == 0, 0.0, above)
    below = jnp.where(row == NTR - 1, 0.0, below)
    outer = jnp.concatenate([above, below, jnp.zeros((CG - 2 * REACH, CG), F32)], axis=0)
    tall = jnp.concatenate([coarse_t[...], jnp.transpose(outer)], axis=1)
    tall_t[...] = tall
    even = is_even("col")
    left, right = tall[:REACH], tall[CG - REACH :]
    send_even[...] = jnp.where(even, right, left)
    send_odd[...] = jnp.where(even, left, right)


def inner_kernel(tall_t, wy_high, wy_low, wx, inner):
    across = weighted(tall_t[...], wy_high[...], wy_low[...])
    inner[...] = jnp.sum(across * wx[:CG, :], axis=0, keepdims=True)


def new_dose(got_even, got_odd, forward, inner, sens, dose_in, wy_high, wy_low, wx):
    col = lax.axis_index("col")
    even = lax.rem(col, 2) == 0
    from_even, from_odd = got_even[...], got_odd[...]
    left = jnp.where(even, from_odd, from_even)
    right = jnp.where(even, from_even, from_odd)
    left = jnp.where(col == 0, 0.0, left)
    right = jnp.where(col == NTC - 1, 0.0, right)
    across = weighted(jnp.concatenate([left, right], axis=0), wy_high[...], wy_low[...])
    background = inner[...] + jnp.sum(across * wx[CG:, :], axis=0, keepdims=True)
    exposure = sens[...] * (forward[...] + BACK_RATIO * background) / (1.0 + BACK_RATIO)
    dose = dose_in[...]
    live = dose > 0.0
    return jnp.where(live, dose * TARGET_LEVEL / jnp.where(live, exposure, 1.0), 0.0), jnp.where(live, exposure, 0.0)


def update_kernel(got_even, got_odd, forward, inner, sens, dose_in, wy_high, wy_low, wx, px, py, dose_out, send_even, send_odd):
    dose, _ = new_dose(got_even, got_odd, forward, inner, sens, dose_in, wy_high, wy_low, wx)
    dose_out[...] = dose
    py_edges = jnp.concatenate([py[:REACH, :], py[CG - REACH :, :]], axis=0).astype(F32)
    row_strips(dose, px[...], py_edges, send_even, send_odd)


def final_kernel(got_even, got_odd, forward, inner, sens, dose_in, wy_high, wy_low, wx, dose_out, exposure_out):
    dose_out[...], exposure_out[...] = new_dose(got_even, got_odd, forward, inner, sens, dose_in, wy_high, wy_low, wx)


def shape(*dims, dtype=F32):
    return jax.ShapeDtypeStruct(dims, dtype)


HBM = pl.BlockSpec(memory_space=pltpu.HBM)
VMEM = pl.BlockSpec(memory_space=pltpu.VMEM)


def call(kernel, outs, vmem=16, ins=None, scratch=()):
    extra = {} if ins is None else {"in_specs": ins}
    return pl.pallas_call(
        kernel,
        out_shape=outs,
        scratch_shapes=scratch,
        compiler_params=pltpu.CompilerParams(vmem_limit_bytes=vmem << 20),
        **extra,
    )


def body(shot_boxes, block_counts, tail_shots, doses, pixel_gain):
    row_even, row_odd, col_even, col_odd = pairings()
    row = shape(1, SLOTS)
    strip = shape(REACH, CG)
    wide = shape(REACH, 2 * CG)
    half = shape(2 * CG, SLOTS, dtype=BF16)
    boxes, dose, strip_even, strip_odd = call(
        start_kernel,
        (shape(4, 1, SLOTS, dtype=jnp.int32), row, strip, strip),
        ins=[HBM] * 4,
        scratch=(pltpu.VMEM((1, NTC), jnp.int32), pltpu.VMEM((1, NTC), jnp.int32), pltpu.VMEM((1, SLOTS), F32), pltpu.SemaphoreType.DMA((4,))),
    )(*[pltpu.with_memory_space_constraint(a, pltpu.HBM) for a in (shot_boxes, block_counts, tail_shots, doses)])
    for sweep in range(ITERS):
        got_odd = lax.ppermute(strip_odd, AXES, row_odd)
        got_even = lax.ppermute(strip_even, AXES, row_even)
        if sweep == 0:
            px, py, coarse_t, early_pairs, gain = call(
                early_kernel,
                (shape(CG, SLOTS, dtype=BF16), shape(CG, SLOTS, dtype=BF16), shape(CG, CG), shape(EARLY, SLOTS), shape(TILE, TILE)),
                ins=[VMEM, VMEM, HBM],
                scratch=(pltpu.SemaphoreType.DMA,),
            )(boxes, dose, pltpu.with_memory_space_constraint(pixel_gain, pltpu.HBM))
        else:
            coarse_t = call(coarse_kernel, shape(CG, CG))(dose, px, py)
        tall_t, wide_even, wide_odd = call(middle_kernel, (shape(CG, 2 * CG), wide, wide))(got_even, got_odd, coarse_t)
        far_odd = lax.ppermute(wide_odd, AXES, col_odd)
        far_even = lax.ppermute(wide_even, AXES, col_even)
        if sweep == 0:
            wy_high, wy_low, wx, late_pairs, sens = call(
                late_kernel, (half, half, shape(CG + 2 * REACH, SLOTS), shape(SLOTS - EARLY, SLOTS), row)
            )(boxes, gain)
        forward = call(forward_kernel, row)(dose, early_pairs, late_pairs)
        inner = call(inner_kernel, row)(tall_t, wy_high, wy_low, wx)
        common = (far_even, far_odd, forward, inner, sens, dose, wy_high, wy_low, wx)
        if sweep < ITERS - 1:
            dose, strip_even, strip_odd = call(update_kernel, (row, strip, strip))(*common, px, py)
    return call(final_kernel, (row, row))(*common)


def solution(mesh):
    placed = (P(None, "row", "col"), P("row", None), P("row", None), P("row", "col"), P("row", "col"))
    return jax.shard_map(body, mesh=mesh, in_specs=placed, out_specs=(P("row", "col"), P("row", "col")), check_vma=False)
```

```python
import math

import jax
import jax.numpy as jnp
from jax import lax
from jax.experimental import pallas as pl
from jax.experimental.pallas import tpu as pltpu
from jax.sharding import PartitionSpec as P


TILE = 512
CG = 128
BLK = 128
CELL = 4
BETA = 16
REACH = 32
SLOTS = 1024
NTR = 8
NTC = 16
FORWARD_RANGE = 4.0
BACK_RATIO = 0.75
TARGET_LEVEL = 1.0
F32 = jnp.float32
BF16 = jnp.bfloat16
AXES = ("row", "col")
NT = (((1,), (1,)), ((), ()))
MAXB = 8
SIDE = CG + REACH
ALL = CG + 2 * REACH


def pairings():
    def number(r, c):
        return r * NTC + c

    def table(partner):
        return [(number(r, c), number(*partner(r, c))) for r in range(NTR) for c in range(NTC)]

    def odd(i):
        return ((i - 1) ^ 1) + 1

    row_even = table(lambda r, c: (r ^ 1, c))
    row_odd = table(lambda r, c: (r, c ^ 1) if r in (0, NTR - 1) else (odd(r), c))
    col_even = table(lambda r, c: (r, c ^ 1))
    col_odd = table(lambda r, c: (r ^ 1, c) if c in (0, NTC - 1) else (r, odd(c)))
    return row_even, row_odd, col_even, col_odd


def two_parts(value):
    high = value.astype(BF16)
    low = (value - high.astype(F32)).astype(BF16)
    return high, low


def stacked_dot(value, other, dims):
    rows = value.shape[0]
    parts = jnp.concatenate(two_parts(value), axis=0)
    both = lax.dot_general(parts, other, dims, preferred_element_type=F32)
    return both[:rows] + both[rows:]


def weighted(columns, high, low):
    first, second = two_parts(columns)
    return jnp.dot(
        jnp.concatenate([first, first, second], axis=1), jnp.concatenate([high, low, high], axis=0), preferred_element_type=F32
    )


def overlap(low_edge, high_edge, cells):
    begin = cells * CELL
    covered = jnp.minimum(high_edge, begin + CELL) - jnp.maximum(low_edge, begin)
    return jnp.maximum(covered, 0).astype(F32) * (1.0 / CELL)


def spread(distance):
    scaled = distance.astype(F32) / BETA
    inside = jnp.abs(distance) <= REACH
    return jnp.where(inside, jnp.exp(-scaled * scaled) / (math.sqrt(math.pi) * BETA), 0.0)


def iota(shape, axis):
    return lax.broadcasted_iota(jnp.int32, shape, axis)


def is_even(axis):
    return lax.rem(lax.axis_index(axis), 2) == 0


def sides(from_even, from_odd):
    col = lax.axis_index("col")
    even = lax.rem(col, 2) == 0
    left = jnp.where(even, from_odd, from_even)
    right = jnp.where(even, from_even, from_odd)
    return jnp.where(col == 0, 0.0, left), jnp.where(col == NTC - 1, 0.0, right)


def outer_rows(from_even, from_odd):
    row = lax.axis_index("row")
    even = lax.rem(row, 2) == 0
    above = jnp.where(even, from_odd, from_even)
    below = jnp.where(even, from_even, from_odd)
    return jnp.concatenate([jnp.where(row == 0, 0.0, above), jnp.where(row == NTR - 1, 0.0, below)], axis=0)


def send_rows(edges, send_even, send_odd):
    even = is_even("row")
    top, bottom = edges[:REACH], edges[REACH:]
    send_even[...] = jnp.where(even, bottom, top)
    send_odd[...] = jnp.where(even, top, bottom)


def boxes_of(tile):
    return [tile[k].astype(jnp.int32) for k in range(4)]


def edge_part(py):
    return jnp.concatenate([py[:REACH, :], py[CG - REACH :, :]], axis=0).astype(F32)


def start_kernel(boxes_in, counts_in, tails_in, doses_in, tile, boxes, counts, tails, doses, arrived):
    copies = [
        pltpu.make_async_copy(source, target, arrived.at[k])
        for k, (source, target) in enumerate(((boxes_in, boxes), (counts_in, counts), (tails_in, tails), (doses_in, doses)))
    ]
    for copy in copies:
        copy.start()
    for copy in copies:
        copy.wait()
    col = lax.axis_index("col")
    totals = (counts[...] - 1) * BLK + tails[...]
    total = jnp.sum(jnp.where(iota((1, NTC), 1) == col, totals, 0), axis=1, keepdims=True)
    live = iota((1, SLOTS), 1) < total
    for k in range(4):
        tile[k] = boxes[k].astype(F32)
    tile[4] = jnp.where(live, doses[...], 0.0)


def as_columns(dose):
    return jnp.transpose(jnp.concatenate([dose[:, k * BLK : (k + 1) * BLK] for k in range(MAXB)], axis=0))


def folded_sum(value):
    return jnp.sum(value.reshape(BLK // 8, 8, SLOTS), axis=0)


def early_kernel(tile, gain_in, px_out, py_out, pairs, told, gain, arrived):
    copy = pltpu.make_async_copy(gain_in, gain, arrived)
    copy.start()
    inverse = 1.0 / FORWARD_RANGE
    box = [tile[k] for k in range(4)]
    centre_x = (box[0] + box[2]) * (0.5 * inverse)
    centre_y = (box[1] + box[3]) * (0.5 * inverse)
    columns = jnp.concatenate([b * inverse for b in box] + [tile[4], jnp.zeros((3, SLOTS), F32)], axis=0)
    total = jnp.zeros((8, SLOTS), F32)
    for at in range(0, SLOTS, BLK):
        side = jnp.transpose(columns[:, at : at + BLK])
        along_x = lax.erf(centre_x - side[:, 0:1]) - lax.erf(centre_x - side[:, 2:3])
        along_y = lax.erf(centre_y - side[:, 1:2]) - lax.erf(centre_y - side[:, 3:4])
        block = (0.25 * along_x) * along_y
        pairs[at : at + BLK, :] = block
        total += folded_sum(side[:, 4:5] * block)
    told[0] = jnp.sum(total, axis=0, keepdims=True)
    boxes = boxes_of(tile)
    px_out[...] = overlap(boxes[0], boxes[2], iota((CG, SLOTS), 0)).astype(BF16)
    py_out[...] = overlap(boxes[1], boxes[3], iota((CG, SLOTS), 0)).astype(BF16)
    pixel_x = (boxes[0] + boxes[2]) // 2
    pixel_y = (boxes[1] + boxes[3]) // 2
    pixels = iota((TILE, SLOTS), 0)
    chosen_x = jnp.where(pixels == pixel_x, 1.0, 0.0).astype(BF16)
    copy.wait()
    picked = stacked_dot(gain[...], chosen_x, (((1,), (0,)), ((), ())))
    told[1] = jnp.sum(jnp.where(pixels == pixel_y, picked, 0.0), axis=0, keepdims=True)


def first_strips_kernel(own, got_even, got_odd, px, py, left_out, right_out, px_left, px_right, send_even, send_odd):
    left, right = sides(got_even[...], got_odd[...])
    left_out[...] = left
    right_out[...] = right
    edge_cells = iota((2 * REACH, SLOTS), 0)
    edge_cells = jnp.where(edge_cells < REACH, edge_cells, edge_cells + (CG - 2 * REACH))
    edges = [stacked_dot(edge_part(py) * own[4], px[...], NT)]
    for tile, px_out in ((left, px_left), (right, px_right)):
        boxes = boxes_of(tile)
        across = overlap(boxes[0], boxes[2], iota((CG, SLOTS), 0)).astype(BF16)
        px_out[...] = across
        edges.append(stacked_dot(overlap(boxes[1], boxes[3], edge_cells) * tile[4], across, NT))
    send_rows(jnp.concatenate([edges[1], edges[0], edges[2]], axis=1), send_even, send_odd)


def strips_kernel(doses, px_left, px, px_right, py_left, py, py_right, send_even, send_odd):
    pieces = ((0, px_left, py_left), (1, px, py), (2, px_right, py_right))
    edges = [stacked_dot(edge_part(down) * doses[k], across[...], NT) for k, across, down in pieces]
    send_rows(jnp.concatenate(edges, axis=1), send_even, send_odd)


def last_strips_kernel(doses, px_left, px, px_right, py_left, py, py_right, send_even, send_odd):
    edges = [
        stacked_dot(edge_part(py) * doses[1], px[...], NT),
        stacked_dot(edge_part(py_left) * doses[0], px_left[CG - REACH :, :], NT),
        stacked_dot(edge_part(py_right) * doses[2], px_right[:REACH, :], NT),
        jnp.zeros((2 * REACH, 2 * CG - ALL), F32),
    ]
    send_rows(jnp.concatenate(edges, axis=1), send_even, send_odd)


def per_tile(left, own, right):
    return (
        jnp.concatenate([left, own[:REACH]], axis=0),
        jnp.concatenate([own, left[CG - REACH :], right[:REACH]], axis=0),
        jnp.concatenate([right, own[CG - REACH :]], axis=0),
    )


def inner_sums(doses, px, py, wy_high, wy_low, wx, inner):
    coarse = [stacked_dot(across.astype(F32) * dose, down, NT) for dose, across, down in zip(doses, px, py)]
    for k, columns in enumerate(per_tile(*coarse)):
        across = weighted(columns, wy_high[k, :CG, :], wy_low[k, :CG, :])
        inner[k] = jnp.sum(across * wx[k][...], axis=0, keepdims=True)


def late_kernel(own, left, right, px_left, px, px_right, py, py_left, py_right, wy_high, wy_low, wx_left, wx, wx_right, inner):
    tiles = (left, own, right)
    boxes = [boxes_of(tile) for tile in tiles]
    y = iota((ALL, SLOTS), 0)
    y = jnp.where(y < CG, y, jnp.where(y < CG + REACH, y - (CG + REACH), y - REACH))
    x = iota((SIDE, SLOTS), 0)
    places = (x, y, jnp.where(x < CG, x, x - (CG + REACH)))
    for k, (box, place, out) in enumerate(zip(boxes, places, (wx_left, wx, wx_right))):
        out[...] = spread((box[0] + box[2]) // (2 * CELL) - place)
        wy_high[k], wy_low[k] = two_parts(spread((box[1] + box[3]) // (2 * CELL) - y))
    for box, out in ((boxes[0], py_left), (boxes[2], py_right)):
        out[...] = overlap(box[1], box[3], iota((CG, SLOTS), 0)).astype(BF16)
    inner_sums(
        [tile[4] for tile in tiles],
        (px_left[...], px[...], px_right[...]),
        (py_left[...], py[...], py_right[...]),
        wy_high,
        wy_low,
        (wx_left, wx, wx_right),
        inner,
    )


def inner_kernel(doses, px_left, px, px_right, py_left, py, py_right, wy_high, wy_low, wx_left, wx, wx_right, inner):
    inner_sums(
        [doses[k] for k in range(3)],
        (px_left[...], px[...], px_right[...]),
        (py_left[...], py[...], py_right[...]),
        wy_high,
        wy_low,
        (wx_left, wx, wx_right),
        inner,
    )


def last_inner_kernel(doses, px_left, px, px_right, py_left, py, py_right, wy_high, wy_low, wx, pairs, inner, forward):
    coarse = jnp.concatenate(
        [
            stacked_dot(px[...].astype(F32) * doses[1], py[...], NT),
            stacked_dot(px_left[CG - REACH :, :].astype(F32) * doses[0], py_left[...], NT),
            stacked_dot(px_right[:REACH, :].astype(F32) * doses[2], py_right[...], NT),
        ],
        axis=0,
    )
    across = weighted(coarse, wy_high[1, :CG, :], wy_low[1, :CG, :])
    inner[...] = jnp.sum(across * wx[...], axis=0, keepdims=True)
    forward[...] = pair_sum(doses[1], pairs)


def pair_sum(dose, pairs):
    columns = as_columns(dose)
    total = jnp.zeros((8, SLOTS), F32)
    for k in range(MAXB):
        total += folded_sum(columns[:, k : k + 1] * pairs[k * BLK : (k + 1) * BLK, :])
    return jnp.sum(total, axis=0, keepdims=True)


def forward_kernel(doses, pairs, told):
    told[0] = pair_sum(doses[1], pairs)


def exposed(dose, sens, forward, background):
    live = dose > 0.0
    exposure = sens * (forward + BACK_RATIO * background) / (1.0 + BACK_RATIO)
    return jnp.where(live, dose * TARGET_LEVEL / jnp.where(live, exposure, 1.0), 0.0), jnp.where(live, exposure, 0.0)


def update(got_even, got_odd, doses, sens, forward, inner, wy_high, wy_low, wx, doses_out):
    outer = outer_rows(got_even[...], got_odd[...])
    outer_t = [jnp.transpose(outer[:, k * CG : (k + 1) * CG]) for k in range(3)]
    for k, columns in enumerate(per_tile(*outer_t)):
        across = weighted(columns, wy_high[k, CG:, :], wy_low[k, CG:, :])
        background = inner[k] + jnp.sum(across * wx[k][...], axis=0, keepdims=True)
        doses_out[k], _ = exposed(doses[k], sens[k], forward[k], background)


def first_update_kernel(
    got_even, got_odd, told, told_even, told_odd, own, left, right, inner, wy_high, wy_low, wx_left, wx, wx_right, doses_out, sens_out
):
    told_left, told_right = sides(told_even[...], told_odd[...])
    forward, sens = zip((told_left[0], told_left[1]), (told[0], told[1]), (told_right[0], told_right[1]))
    for k in range(3):
        sens_out[k] = sens[k]
    update(got_even, got_odd, (left[4], own[4], right[4]), sens, forward, inner, wy_high, wy_low, (wx_left, wx, wx_right), doses_out)


def update_kernel(got_even, got_odd, told, told_even, told_odd, doses, sens, inner, wy_high, wy_low, wx_left, wx, wx_right, doses_out):
    told_left, told_right = sides(told_even[...], told_odd[...])
    update(
        got_even,
        got_odd,
        [doses[k] for k in range(3)],
        [sens[k] for k in range(3)],
        (told_left[0], told[0], told_right[0]),
        inner,
        wy_high,
        wy_low,
        (wx_left, wx, wx_right),
        doses_out,
    )


def final_kernel(got_even, got_odd, doses, sens, inner, forward, wy_high, wy_low, wx, dose_out, exposure_out):
    outer = outer_rows(got_even[...], got_odd[...])
    columns = jnp.concatenate([jnp.transpose(outer[:, :CG]), jnp.transpose(outer[:, CG:])[: 2 * REACH]], axis=0)
    across = weighted(columns, wy_high[1, CG:, :], wy_low[1, CG:, :])
    background = inner[...] + jnp.sum(across * wx[...], axis=0, keepdims=True)
    dose_out[...], exposure_out[...] = exposed(doses[1], sens[1], forward[...], background)


def shape(*dims, dtype=F32):
    return jax.ShapeDtypeStruct(dims, dtype)


HBM = pl.BlockSpec(memory_space=pltpu.HBM)
VMEM = pl.BlockSpec(memory_space=pltpu.VMEM)


def call(kernel, outs, vmem=24, ins=None, scratch=()):
    extra = {} if ins is None else {"in_specs": ins}
    return pl.pallas_call(
        kernel,
        out_shape=outs,
        scratch_shapes=scratch,
        compiler_params=pltpu.CompilerParams(vmem_limit_bytes=vmem << 20),
        **extra,
    )


def in_hbm(*arrays):
    return [pltpu.with_memory_space_constraint(array, pltpu.HBM) for array in arrays]


def send(value, table):
    return lax.ppermute(value, AXES, table)


def body(shot_boxes, block_counts, tail_shots, doses, pixel_gain):
    row_even, row_odd, col_even, col_odd = pairings()
    row = shape(1, SLOTS)
    rows = shape(3, 1, SLOTS)
    cover = shape(CG, SLOTS, dtype=BF16)
    tile = shape(5, 1, SLOTS)
    weights = shape(3, ALL, SLOTS, dtype=BF16)
    strip = shape(REACH, 3 * CG)
    short = shape(REACH, 2 * CG)
    own = call(
        start_kernel,
        tile,
        ins=[HBM] * 4,
        scratch=(
            pltpu.VMEM((4, 1, SLOTS), jnp.int32),
            pltpu.VMEM((1, NTC), jnp.int32),
            pltpu.VMEM((1, NTC), jnp.int32),
            pltpu.VMEM((1, SLOTS), F32),
            pltpu.SemaphoreType.DMA((4,)),
        ),
    )(*in_hbm(shot_boxes, block_counts, tail_shots, doses))
    far_odd = send(own, col_odd)
    far_even = send(own, col_even)
    px, py, pairs, told = call(
        early_kernel,
        (cover, cover, shape(SLOTS, SLOTS), shape(2, 1, SLOTS)),
        ins=[VMEM, HBM],
        scratch=(pltpu.VMEM((TILE, TILE), F32), pltpu.SemaphoreType.DMA),
    )(own, *in_hbm(pixel_gain))
    told_odd = send(told, col_odd)
    left, right, px_left, px_right, strip_even, strip_odd = call(
        first_strips_kernel, (tile, tile, cover, cover, strip, strip)
    )(own, far_even, far_odd, px, py)
    got_odd = send(strip_odd, row_odd)
    got_even = send(strip_even, row_even)
    told_even = send(told, col_even)
    py_left, py_right, wy_high, wy_low, wx_left, wx, wx_right, inner = call(
        late_kernel, (cover, cover, weights, weights, shape(SIDE, SLOTS), shape(ALL, SLOTS), shape(SIDE, SLOTS), rows)
    )(own, left, right, px_left, px, px_right, py)
    covers = (px_left, px, px_right, py_left, py, py_right)
    weighing = (wy_high, wy_low, wx_left, wx, wx_right)
    doses3, sens = call(first_update_kernel, (rows, rows))(
        got_even, got_odd, told, told_even, told_odd, own, left, right, inner, *weighing
    )
    told = call(forward_kernel, shape(1, 1, SLOTS))(doses3, pairs)
    told_odd = send(told, col_odd)
    strip_even, strip_odd = call(strips_kernel, (strip, strip))(doses3, *covers)
    got_odd = send(strip_odd, row_odd)
    got_even = send(strip_even, row_even)
    told_even = send(told, col_even)
    inner = call(inner_kernel, rows)(doses3, *covers, *weighing)
    doses3 = call(update_kernel, rows)(got_even, got_odd, told, told_even, told_odd, doses3, sens, inner, *weighing)
    strip_even, strip_odd = call(last_strips_kernel, (short, short))(doses3, *covers)
    got_odd = send(strip_odd, row_odd)
    got_even = send(strip_even, row_even)
    inner, forward = call(last_inner_kernel, (row, row))(doses3, *covers, wy_high, wy_low, wx, pairs)
    return call(final_kernel, (row, row))(got_even, got_odd, doses3, sens, inner, forward, wy_high, wy_low, wx)


def solution(mesh):
    placed = (P(None, "row", "col"), P("row", None), P("row", None), P("row", "col"), P("row", "col"))
    return jax.shard_map(body, mesh=mesh, in_specs=placed, out_specs=(P("row", "col"), P("row", "col")), check_vma=False)
```

```python
import math

import jax
import jax.numpy as jnp
from jax import lax
from jax.experimental import pallas as pl
from jax.experimental.pallas import tpu as pltpu
from jax.sharding import PartitionSpec as P


TILE = 512
CG = 128
BLK = 128
CELL = 4
BETA = 16
REACH = 32
SLOTS = 1024
NTR = 8
NTC = 16
FORWARD_RANGE = 4.0
BACK_RATIO = 0.75
TARGET_LEVEL = 1.0
F32 = jnp.float32
BF16 = jnp.bfloat16
AXES = ("row", "col")
NT = (((1,), (1,)), ((), ()))
MAXB = 8
SIDE = CG + REACH
ALL = CG + 2 * REACH


def pairings():
    def number(r, c):
        return r * NTC + c

    def table(partner):
        return [(number(r, c), number(*partner(r, c))) for r in range(NTR) for c in range(NTC)]

    def odd(i):
        return ((i - 1) ^ 1) + 1

    row_even = table(lambda r, c: (r ^ 1, c))
    row_odd = table(lambda r, c: (r, c ^ 1) if r in (0, NTR - 1) else (odd(r), c))
    col_even = table(lambda r, c: (r, c ^ 1))
    col_odd = table(lambda r, c: (r ^ 1, c) if c in (0, NTC - 1) else (r, odd(c)))
    return row_even, row_odd, col_even, col_odd


def two_parts(value):
    high = value.astype(BF16)
    low = (value - high.astype(F32)).astype(BF16)
    return high, low


def stacked_dot(value, other, dims):
    rows = value.shape[0]
    parts = jnp.concatenate(two_parts(value), axis=0)
    both = lax.dot_general(parts, other, dims, preferred_element_type=F32)
    return both[:rows] + both[rows:]


def weighted(columns, high, low):
    first, second = two_parts(columns)
    return jnp.dot(
        jnp.concatenate([first, first, second], axis=1), jnp.concatenate([high, low, high], axis=0), preferred_element_type=F32
    )


def overlap(low_edge, high_edge, cells):
    begin = cells * CELL
    covered = jnp.minimum(high_edge, begin + CELL) - jnp.maximum(low_edge, begin)
    return jnp.maximum(covered, 0.0) * (1.0 / CELL)


def gauss(cells, places):
    rate = math.sqrt(math.log2(math.e)) / BETA
    level = -math.log2(math.sqrt(math.pi) * BETA)
    scaled = cells * rate - places.astype(F32) * rate
    square = scaled * scaled
    return jnp.where(square <= (rate * (REACH + 0.5)) ** 2, jnp.exp2(level - square), 0.0)


def iota(shape, axis):
    return lax.broadcasted_iota(jnp.int32, shape, axis)


def is_even(axis):
    return lax.rem(lax.axis_index(axis), 2) == 0


def sides(from_even, from_odd):
    col = lax.axis_index("col")
    even = lax.rem(col, 2) == 0
    left = jnp.where(even, from_odd, from_even)
    right = jnp.where(even, from_even, from_odd)
    return jnp.where(col == 0, 0.0, left), jnp.where(col == NTC - 1, 0.0, right)


def outer_rows(from_even, from_odd):
    row = lax.axis_index("row")
    even = lax.rem(row, 2) == 0
    above = jnp.where(even, from_odd, from_even)
    below = jnp.where(even, from_even, from_odd)
    return jnp.concatenate([jnp.where(row == 0, 0.0, above), jnp.where(row == NTR - 1, 0.0, below)], axis=0)


def send_rows(edges, send_even, send_odd):
    even = is_even("row")
    top, bottom = edges[:REACH], edges[REACH:]
    send_even[...] = jnp.where(even, bottom, top)
    send_odd[...] = jnp.where(even, top, bottom)


def boxes_of(tile):
    return [tile[k].astype(jnp.int32) for k in range(4)]


def cells_from(first, count):
    return (iota((count, SLOTS), 0) + first).astype(F32)


def edge_part(py):
    return jnp.concatenate([py[:REACH, :], py[CG - REACH :, :]], axis=0).astype(F32)


def start_kernel(boxes_in, counts_in, tails_in, doses_in, tile, boxes, counts, tails, doses, arrived):
    copies = [
        pltpu.make_async_copy(source, target, arrived.at[k])
        for k, (source, target) in enumerate(((boxes_in, boxes), (counts_in, counts), (tails_in, tails), (doses_in, doses)))
    ]
    for copy in copies:
        copy.start()
    for copy in copies:
        copy.wait()
    col = lax.axis_index("col")
    totals = (counts[...] - 1) * BLK + tails[...]
    total = jnp.sum(jnp.where(iota((1, NTC), 1) == col, totals, 0), axis=1, keepdims=True)
    live = iota((1, SLOTS), 1) < total
    for k in range(4):
        tile[k] = boxes[k].astype(F32)
    tile[4] = jnp.where(live, doses[...], 0.0)


def as_columns(dose):
    return jnp.transpose(jnp.concatenate([dose[:, k * BLK : (k + 1) * BLK] for k in range(MAXB)], axis=0))


def folded_sum(value):
    return jnp.sum(value.reshape(BLK // 8, 8, SLOTS), axis=0)


def early_kernel(tile, gain_in, px_out, py_out, pairs, told, gain, gain_parts, picked, chosen_x, arrived):
    copy = pltpu.make_async_copy(gain_in, gain, arrived)
    copy.start()
    boxes = boxes_of(tile)
    pixel_x = (boxes[0] + boxes[2]) // 2
    pixel_y = (boxes[1] + boxes[3]) // 2
    for at in range(0, TILE, 16):
        chosen_x[at : at + 16, :] = jnp.where(iota((16, SLOTS), 0) + at == pixel_x, 1.0, 0.0).astype(BF16)
    inverse = 1.0 / FORWARD_RANGE
    box = [tile[k] for k in range(4)]
    centre_x = jnp.broadcast_to((box[0] + box[2]) * (0.5 * inverse), (8, SLOTS))
    centre_y = jnp.broadcast_to((box[1] + box[3]) * (0.5 * inverse), (8, SLOTS))
    columns = jnp.concatenate([b * inverse for b in box] + [tile[4], jnp.zeros((3, SLOTS), F32)], axis=0)
    total = jnp.zeros((8, SLOTS), F32)
    for block in range(MAXB):
        at = block * BLK
        if block == 3:
            copy.wait()
            high, low = two_parts(gain[...])
            gain_parts[...] = jnp.concatenate([high, low], axis=1)
        if block >= 3 and block < 7:
            lanes = slice((block - 3) * 256, (block - 2) * 256)
            chosen = chosen_x[:, lanes]
            picked[...] = jnp.dot(gain_parts[...], jnp.concatenate([chosen, chosen], axis=0), preferred_element_type=F32)
        side = jnp.transpose(columns[:, at : at + BLK])
        for down in range(0, BLK, 8):
            low_x, low_y, high_x, high_y, dose = [side[down : down + 8, k : k + 1] for k in range(5)]
            along_x = lax.erf(centre_x - low_x) - lax.erf(centre_x - high_x)
            along_y = lax.erf(centre_y - low_y) - lax.erf(centre_y - high_y)
            values = (0.25 * along_x) * along_y
            pairs[at + down : at + down + 8, :] = values
            total += dose * values
        if block >= 3 and block < 7:
            found = jnp.zeros((8, 256), F32)
            for row in range(0, TILE, 8):
                found += jnp.where(iota((8, 256), 0) + row == pixel_y[:, lanes], picked[row : row + 8, :], 0.0)
            told[1, :, lanes] = jnp.sum(found, axis=0, keepdims=True)
        if block < 3:
            for first in range(block * 48, min(block * 48 + 48, CG), 16):
                px_out[first : first + 16, :] = overlap(box[0], box[2], cells_from(first, 16)).astype(BF16)
                py_out[first : first + 16, :] = overlap(box[1], box[3], cells_from(first, 16)).astype(BF16)
    told[0] = jnp.sum(total, axis=0, keepdims=True)


def first_strips_kernel(own, got_even, got_odd, px, py, left_out, right_out, px_left, px_right, send_even, send_odd):
    left, right = sides(got_even[...], got_odd[...])
    left_out[...] = left
    right_out[...] = right
    edge_cells = jnp.concatenate([cells_from(0, REACH), cells_from(CG - REACH, REACH)], axis=0)
    edges = [stacked_dot(edge_part(py) * own[4], px[...], NT)]
    for tile, px_out in ((left, px_left), (right, px_right)):
        across = overlap(tile[0], tile[2], cells_from(0, CG)).astype(BF16)
        px_out[...] = across
        edges.append(stacked_dot(overlap(tile[1], tile[3], edge_cells) * tile[4], across, NT))
    send_rows(jnp.concatenate([edges[1], edges[0], edges[2]], axis=1), send_even, send_odd)


def strips_kernel(doses, px_left, px, px_right, py_left, py, py_right, send_even, send_odd):
    pieces = ((0, px_left, py_left), (1, px, py), (2, px_right, py_right))
    edges = [stacked_dot(edge_part(down) * doses[k], across[...], NT) for k, across, down in pieces]
    send_rows(jnp.concatenate(edges, axis=1), send_even, send_odd)


def last_strips_kernel(doses, px_left, px, px_right, py_left, py, py_right, send_even, send_odd):
    edges = [
        stacked_dot(edge_part(py) * doses[1], px[...], NT),
        stacked_dot(edge_part(py_left) * doses[0], px_left[CG - REACH :, :], NT),
        stacked_dot(edge_part(py_right) * doses[2], px_right[:REACH, :], NT),
        jnp.zeros((2 * REACH, 2 * CG - ALL), F32),
    ]
    send_rows(jnp.concatenate(edges, axis=1), send_even, send_odd)


def per_tile(left, own, right):
    return (
        jnp.concatenate([left, own[:REACH]], axis=0),
        jnp.concatenate([own, left[CG - REACH :], right[:REACH]], axis=0),
        jnp.concatenate([right, own[CG - REACH :]], axis=0),
    )


def inner_sums(doses, px, py, wy_high, wy_low, wx, inner):
    coarse = [stacked_dot(across.astype(F32) * dose, down, NT) for dose, across, down in zip(doses, px, py)]
    for k, columns in enumerate(per_tile(*coarse)):
        across = weighted(columns, wy_high[k, :CG, :], wy_low[k, :CG, :])
        inner[k] = jnp.sum(across * wx[k][...], axis=0, keepdims=True)


def late_kernel(own, left, right, px_left, px, px_right, py, py_left, py_right, wy_high, wy_low, wx_left, wx, wx_right, inner):
    tiles = (left, own, right)
    boxes = [boxes_of(tile) for tile in tiles]
    cells = [[((box[k] + box[k + 2]) // (2 * CELL)).astype(F32) for k in range(2)] for box in boxes]
    for at in range(0, ALL, 16):
        apart = CG + REACH if CG <= at < CG + REACH else (REACH if at >= CG + REACH else 0)
        outer = iota((16, 1), 0) + (at - apart)
        for k, box_cells in enumerate(cells):
            wy_high[k, at : at + 16, :], wy_low[k, at : at + 16, :] = two_parts(gauss(box_cells[1], outer))
        wx[at : at + 16, :] = gauss(cells[1][0], outer)
        if at < SIDE:
            columns = iota((16, 1), 0) + at
            wx_left[at : at + 16, :] = gauss(cells[0][0], columns)
            wx_right[at : at + 16, :] = gauss(cells[2][0], columns if at < CG else columns - SIDE)
    for tile, out in ((left, py_left), (right, py_right)):
        out[...] = overlap(tile[1], tile[3], cells_from(0, CG)).astype(BF16)
    inner_sums(
        [tile[4] for tile in tiles],
        (px_left[...], px[...], px_right[...]),
        (py_left[...], py[...], py_right[...]),
        wy_high,
        wy_low,
        (wx_left, wx, wx_right),
        inner,
    )


def inner_kernel(doses, px_left, px, px_right, py_left, py, py_right, wy_high, wy_low, wx_left, wx, wx_right, inner):
    inner_sums(
        [doses[k] for k in range(3)],
        (px_left[...], px[...], px_right[...]),
        (py_left[...], py[...], py_right[...]),
        wy_high,
        wy_low,
        (wx_left, wx, wx_right),
        inner,
    )


def last_inner_kernel(doses, px_left, px, px_right, py_left, py, py_right, wy_high, wy_low, wx, pairs, inner, forward):
    coarse = jnp.concatenate(
        [
            stacked_dot(px[...].astype(F32) * doses[1], py[...], NT),
            stacked_dot(px_left[CG - REACH :, :].astype(F32) * doses[0], py_left[...], NT),
            stacked_dot(px_right[:REACH, :].astype(F32) * doses[2], py_right[...], NT),
        ],
        axis=0,
    )
    across = weighted(coarse, wy_high[1, :CG, :], wy_low[1, :CG, :])
    inner[...] = jnp.sum(across * wx[...], axis=0, keepdims=True)
    forward[...] = pair_sum(doses[1], pairs)


def pair_sum(dose, pairs):
    columns = as_columns(dose)
    total = jnp.zeros((8, SLOTS), F32)
    for k in range(MAXB):
        total += folded_sum(columns[:, k : k + 1] * pairs[k * BLK : (k + 1) * BLK, :])
    return jnp.sum(total, axis=0, keepdims=True)


def forward_kernel(doses, pairs, told):
    told[0] = pair_sum(doses[1], pairs)


def exposed(dose, sens, forward, background):
    live = dose > 0.0
    exposure = sens * (forward + BACK_RATIO * background) / (1.0 + BACK_RATIO)
    return jnp.where(live, dose * TARGET_LEVEL / jnp.where(live, exposure, 1.0), 0.0), jnp.where(live, exposure, 0.0)


def update(got_even, got_odd, doses, sens, forward, inner, wy_high, wy_low, wx, doses_out):
    outer = outer_rows(got_even[...], got_odd[...])
    outer_t = [jnp.transpose(outer[:, k * CG : (k + 1) * CG]) for k in range(3)]
    for k, columns in enumerate(per_tile(*outer_t)):
        across = weighted(columns, wy_high[k, CG:, :], wy_low[k, CG:, :])
        background = inner[k] + jnp.sum(across * wx[k][...], axis=0, keepdims=True)
        doses_out[k], _ = exposed(doses[k], sens[k], forward[k], background)


def first_update_kernel(
    got_even, got_odd, told, told_even, told_odd, own, left, right, inner, wy_high, wy_low, wx_left, wx, wx_right, doses_out, sens_out
):
    told_left, told_right = sides(told_even[...], told_odd[...])
    forward, sens = zip((told_left[0], told_left[1]), (told[0], told[1]), (told_right[0], told_right[1]))
    for k in range(3):
        sens_out[k] = sens[k]
    update(got_even, got_odd, (left[4], own[4], right[4]), sens, forward, inner, wy_high, wy_low, (wx_left, wx, wx_right), doses_out)


def update_kernel(got_even, got_odd, told, told_even, told_odd, doses, sens, inner, wy_high, wy_low, wx_left, wx, wx_right, doses_out):
    told_left, told_right = sides(told_even[...], told_odd[...])
    update(
        got_even,
        got_odd,
        [doses[k] for k in range(3)],
        [sens[k] for k in range(3)],
        (told_left[0], told[0], told_right[0]),
        inner,
        wy_high,
        wy_low,
        (wx_left, wx, wx_right),
        doses_out,
    )


def final_kernel(got_even, got_odd, doses, sens, inner, forward, wy_high, wy_low, wx, dose_out, exposure_out):
    outer = outer_rows(got_even[...], got_odd[...])
    columns = jnp.concatenate([jnp.transpose(outer[:, :CG]), jnp.transpose(outer[:, CG:])[: 2 * REACH]], axis=0)
    across = weighted(columns, wy_high[1, CG:, :], wy_low[1, CG:, :])
    background = inner[...] + jnp.sum(across * wx[...], axis=0, keepdims=True)
    dose_out[...], exposure_out[...] = exposed(doses[1], sens[1], forward[...], background)


def shape(*dims, dtype=F32):
    return jax.ShapeDtypeStruct(dims, dtype)


HBM = pl.BlockSpec(memory_space=pltpu.HBM)
VMEM = pl.BlockSpec(memory_space=pltpu.VMEM)


def call(kernel, outs, vmem=24, ins=None, scratch=()):
    extra = {} if ins is None else {"in_specs": ins}
    return pl.pallas_call(
        kernel,
        out_shape=outs,
        scratch_shapes=scratch,
        compiler_params=pltpu.CompilerParams(vmem_limit_bytes=vmem << 20),
        **extra,
    )


def in_hbm(*arrays):
    return [pltpu.with_memory_space_constraint(array, pltpu.HBM) for array in arrays]


def send(value, table):
    return lax.ppermute(value, AXES, table)


def body(shot_boxes, block_counts, tail_shots, doses, pixel_gain):
    row_even, row_odd, col_even, col_odd = pairings()
    row = shape(1, SLOTS)
    rows = shape(3, 1, SLOTS)
    cover = shape(CG, SLOTS, dtype=BF16)
    tile = shape(5, 1, SLOTS)
    weights = shape(3, ALL, SLOTS, dtype=BF16)
    strip = shape(REACH, 3 * CG)
    short = shape(REACH, 2 * CG)
    own = call(
        start_kernel,
        tile,
        ins=[HBM] * 4,
        scratch=(
            pltpu.VMEM((4, 1, SLOTS), jnp.int32),
            pltpu.VMEM((1, NTC), jnp.int32),
            pltpu.VMEM((1, NTC), jnp.int32),
            pltpu.VMEM((1, SLOTS), F32),
            pltpu.SemaphoreType.DMA((4,)),
        ),
    )(*in_hbm(shot_boxes, block_counts, tail_shots, doses))
    far_odd = send(own, col_odd)
    far_even = send(own, col_even)
    px, py, pairs, told = call(
        early_kernel,
        (cover, cover, shape(SLOTS, SLOTS), shape(2, 1, SLOTS)),
        ins=[VMEM, HBM],
        scratch=(
            pltpu.VMEM((TILE, TILE), F32),
            pltpu.VMEM((TILE, 2 * TILE), BF16),
            pltpu.VMEM((TILE, 256), F32),
            pltpu.VMEM((TILE, SLOTS), BF16),
            pltpu.SemaphoreType.DMA,
        ),
    )(own, *in_hbm(pixel_gain))
    told_odd = send(told, col_odd)
    left, right, px_left, px_right, strip_even, strip_odd = call(
        first_strips_kernel, (tile, tile, cover, cover, strip, strip)
    )(own, far_even, far_odd, px, py)
    got_odd = send(strip_odd, row_odd)
    got_even = send(strip_even, row_even)
    told_even = send(told, col_even)
    py_left, py_right, wy_high, wy_low, wx_left, wx, wx_right, inner = call(
        late_kernel, (cover, cover, weights, weights, shape(SIDE, SLOTS), shape(ALL, SLOTS), shape(SIDE, SLOTS), rows)
    )(own, left, right, px_left, px, px_right, py)
    covers = (px_left, px, px_right, py_left, py, py_right)
    weighing = (wy_high, wy_low, wx_left, wx, wx_right)
    doses3, sens = call(first_update_kernel, (rows, rows))(
        got_even, got_odd, told, told_even, told_odd, own, left, right, inner, *weighing
    )
    told = call(forward_kernel, shape(1, 1, SLOTS))(doses3, pairs)
    told_odd = send(told, col_odd)
    strip_even, strip_odd = call(strips_kernel, (strip, strip))(doses3, *covers)
    got_odd = send(strip_odd, row_odd)
    got_even = send(strip_even, row_even)
    told_even = send(told, col_even)
    inner = call(inner_kernel, rows)(doses3, *covers, *weighing)
    doses3 = call(update_kernel, rows)(got_even, got_odd, told, told_even, told_odd, doses3, sens, inner, *weighing)
    strip_even, strip_odd = call(last_strips_kernel, (short, short))(doses3, *covers)
    got_odd = send(strip_odd, row_odd)
    got_even = send(strip_even, row_even)
    inner, forward = call(last_inner_kernel, (row, row))(doses3, *covers, wy_high, wy_low, wx, pairs)
    return call(final_kernel, (row, row))(got_even, got_odd, doses3, sens, inner, forward, wy_high, wy_low, wx)


def solution(mesh):
    placed = (P(None, "row", "col"), P("row", None), P("row", None), P("row", "col"), P("row", "col"))
    return jax.shard_map(body, mesh=mesh, in_specs=placed, out_specs=(P("row", "col"), P("row", "col")), check_vma=False)
```

```python
import math

import jax
import jax.numpy as jnp
from jax import lax
from jax.experimental import pallas as pl
from jax.experimental.pallas import tpu as pltpu
from jax.sharding import PartitionSpec as P


TILE = 512
CG = 128
BLK = 128
CELL = 4
BETA = 16
REACH = 32
SLOTS = 1024
NTR = 8
NTC = 16
FORWARD_RANGE = 4.0
BACK_RATIO = 0.75
TARGET_LEVEL = 1.0
F32 = jnp.float32
BF16 = jnp.bfloat16
AXES = ("row", "col")
NT = (((1,), (1,)), ((), ()))
MAXB = 8
SIDE = CG + REACH
ALL = CG + 2 * REACH


def pairings():
    def number(r, c):
        return r * NTC + c

    def table(partner):
        return [(number(r, c), number(*partner(r, c))) for r in range(NTR) for c in range(NTC)]

    def odd(i):
        return ((i - 1) ^ 1) + 1

    row_even = table(lambda r, c: (r ^ 1, c))
    row_odd = table(lambda r, c: (r, c ^ 1) if r in (0, NTR - 1) else (odd(r), c))
    col_even = table(lambda r, c: (r, c ^ 1))
    col_odd = table(lambda r, c: (r ^ 1, c) if c in (0, NTC - 1) else (r, odd(c)))
    return row_even, row_odd, col_even, col_odd


def two_parts(value):
    high = value.astype(BF16)
    low = (value - high.astype(F32)).astype(BF16)
    return high, low


def stacked_dot(value, other, dims):
    rows = value.shape[0]
    parts = jnp.concatenate(two_parts(value), axis=0)
    both = lax.dot_general(parts, other, dims, preferred_element_type=F32)
    return both[:rows] + both[rows:]


def weighted(columns, high, low):
    first, second = two_parts(columns)
    return jnp.dot(
        jnp.concatenate([first, first, second], axis=1), jnp.concatenate([high, low, high], axis=0), preferred_element_type=F32
    )


def overlap(low_edge, high_edge, cells):
    begin = cells * CELL
    covered = jnp.minimum(high_edge, begin + CELL) - jnp.maximum(low_edge, begin)
    return jnp.maximum(covered, 0.0) * (1.0 / CELL)


def gauss(cells, places):
    rate = math.sqrt(math.log2(math.e)) / BETA
    level = -math.log2(math.sqrt(math.pi) * BETA)
    scaled = cells * rate - places.astype(F32) * rate
    square = scaled * scaled
    return jnp.where(square <= (rate * (REACH + 0.5)) ** 2, jnp.exp2(level - square), 0.0)


def iota(shape, axis):
    return lax.broadcasted_iota(jnp.int32, shape, axis)


def is_even(axis):
    return lax.rem(lax.axis_index(axis), 2) == 0


def sides(from_even, from_odd):
    col = lax.axis_index("col")
    even = lax.rem(col, 2) == 0
    left = jnp.where(even, from_odd, from_even)
    right = jnp.where(even, from_even, from_odd)
    return jnp.where(col == 0, 0.0, left), jnp.where(col == NTC - 1, 0.0, right)


def outer_rows(from_even, from_odd):
    row = lax.axis_index("row")
    even = lax.rem(row, 2) == 0
    above = jnp.where(even, from_odd, from_even)
    below = jnp.where(even, from_even, from_odd)
    return jnp.concatenate([jnp.where(row == 0, 0.0, above), jnp.where(row == NTR - 1, 0.0, below)], axis=0)


def send_rows(edges, send_even, send_odd):
    even = is_even("row")
    top, bottom = edges[:REACH], edges[REACH:]
    send_even[...] = jnp.where(even, bottom, top)
    send_odd[...] = jnp.where(even, top, bottom)


def boxes_of(tile):
    return [tile[k].astype(jnp.int32) for k in range(4)]


def cells_from(first, count):
    return (iota((count, SLOTS), 0) + first).astype(F32)


def edge_part(py):
    return jnp.concatenate([py[:REACH, :], py[CG - REACH :, :]], axis=0).astype(F32)


def start_kernel(boxes_in, counts_in, tails_in, doses_in, tile, boxes, counts, tails, doses, arrived):
    copies = [
        pltpu.make_async_copy(source, target, arrived.at[k])
        for k, (source, target) in enumerate(((boxes_in, boxes), (counts_in, counts), (tails_in, tails), (doses_in, doses)))
    ]
    for copy in copies:
        copy.start()
    for copy in copies:
        copy.wait()
    col = lax.axis_index("col")
    totals = (counts[...] - 1) * BLK + tails[...]
    total = jnp.sum(jnp.where(iota((1, NTC), 1) == col, totals, 0), axis=1, keepdims=True)
    live = iota((1, SLOTS), 1) < total
    for k in range(4):
        tile[k] = boxes[k].astype(F32)
    tile[4] = jnp.where(live, doses[...], 0.0)


def as_columns(dose):
    return jnp.transpose(jnp.concatenate([dose[:, k * BLK : (k + 1) * BLK] for k in range(MAXB)], axis=0))


def folded_sum(value):
    return jnp.sum(value.reshape(BLK // 8, 8, SLOTS), axis=0)


def early_kernel(tile, gain_in, px_out, py_out, pairs, told, gain, gain_parts, picked, chosen_x, arrived):
    copy = pltpu.make_async_copy(gain_in, gain, arrived)
    copy.start()
    boxes = boxes_of(tile)
    pixel_x = (boxes[0] + boxes[2]) // 2
    pixel_y = (boxes[1] + boxes[3]) // 2
    for at in range(0, TILE, 16):
        chosen_x[at : at + 16, :] = jnp.where(iota((16, SLOTS), 0) + at == pixel_x, 1.0, 0.0).astype(BF16)
    inverse = 1.0 / FORWARD_RANGE
    box = [tile[k] for k in range(4)]
    centre_x = jnp.broadcast_to((box[0] + box[2]) * (0.5 * inverse), (8, SLOTS))
    centre_y = jnp.broadcast_to((box[1] + box[3]) * (0.5 * inverse), (8, SLOTS))
    columns = jnp.concatenate([b * inverse for b in box] + [tile[4], jnp.zeros((3, SLOTS), F32)], axis=0)
    total = jnp.zeros((8, SLOTS), F32)
    for block in range(MAXB):
        at = block * BLK
        if block == 3:
            copy.wait()
            high, low = two_parts(gain[...])
            gain_parts[...] = jnp.concatenate([high, low], axis=1)
        if block >= 3 and block < 7:
            lanes = slice((block - 3) * 256, (block - 2) * 256)
            chosen = chosen_x[:, lanes]
            picked[...] = jnp.dot(gain_parts[...], jnp.concatenate([chosen, chosen], axis=0), preferred_element_type=F32)
        side = jnp.transpose(columns[:, at : at + BLK])
        for down in range(0, BLK, 8):
            low_x, low_y, high_x, high_y, dose = [side[down : down + 8, k : k + 1] for k in range(5)]
            along_x = lax.erf(centre_x - low_x) - lax.erf(centre_x - high_x)
            along_y = lax.erf(centre_y - low_y) - lax.erf(centre_y - high_y)
            values = (0.25 * along_x) * along_y
            pairs[at + down : at + down + 8, :] = values
            total += dose * values
        if block >= 3 and block < 7:
            found = jnp.zeros((8, 256), F32)
            for row in range(0, TILE, 8):
                found += jnp.where(iota((8, 256), 0) + row == pixel_y[:, lanes], picked[row : row + 8, :], 0.0)
            told[1, :, lanes] = jnp.sum(found, axis=0, keepdims=True)
        if block < 3:
            for first in range(block * 48, min(block * 48 + 48, CG), 16):
                px_out[first : first + 16, :] = overlap(box[0], box[2], cells_from(first, 16)).astype(BF16)
                py_out[first : first + 16, :] = overlap(box[1], box[3], cells_from(first, 16)).astype(BF16)
    told[0] = jnp.sum(total, axis=0, keepdims=True)


def first_strips_kernel(own, got_even, got_odd, px, py, left_out, right_out, px_left, px_right, send_even, send_odd):
    left, right = sides(got_even[...], got_odd[...])
    left_out[...] = left
    right_out[...] = right
    edge_cells = jnp.concatenate([cells_from(0, REACH), cells_from(CG - REACH, REACH)], axis=0)
    edges = [stacked_dot(edge_part(py) * own[4], px[...], NT)]
    for tile, px_out in ((left, px_left), (right, px_right)):
        across = overlap(tile[0], tile[2], cells_from(0, CG)).astype(BF16)
        px_out[...] = across
        edges.append(stacked_dot(overlap(tile[1], tile[3], edge_cells) * tile[4], across, NT))
    send_rows(jnp.concatenate([edges[1], edges[0], edges[2]], axis=1), send_even, send_odd)


def strips(doses, px, py, send_even, send_odd):
    edges = [stacked_dot(edge_part(down) * dose, across[...], NT) for dose, across, down in zip(doses, px, py)]
    send_rows(jnp.concatenate(edges, axis=1), send_even, send_odd)


def last_strips(doses, px, py, send_even, send_odd):
    edges = [
        stacked_dot(edge_part(py[1]) * doses[1], px[1][...], NT),
        stacked_dot(edge_part(py[0]) * doses[0], px[0][CG - REACH :, :], NT),
        stacked_dot(edge_part(py[2]) * doses[2], px[2][:REACH, :], NT),
        jnp.zeros((2 * REACH, 2 * CG - ALL), F32),
    ]
    send_rows(jnp.concatenate(edges, axis=1), send_even, send_odd)


def per_tile(left, own, right):
    return (
        jnp.concatenate([left, own[:REACH]], axis=0),
        jnp.concatenate([own, left[CG - REACH :], right[:REACH]], axis=0),
        jnp.concatenate([right, own[CG - REACH :]], axis=0),
    )


def inner_sums(doses, px, py, wy_high, wy_low, wx, inner):
    coarse = [stacked_dot(across.astype(F32) * dose, down, NT) for dose, across, down in zip(doses, px, py)]
    for k, columns in enumerate(per_tile(*coarse)):
        across = weighted(columns, wy_high[k, :CG, :], wy_low[k, :CG, :])
        inner[k] = jnp.sum(across * wx[k][...], axis=0, keepdims=True)


def late_kernel(own, left, right, px_left, px, px_right, py, py_left, py_right, wy_high, wy_low, wx_left, wx, wx_right, inner):
    tiles = (left, own, right)
    boxes = [boxes_of(tile) for tile in tiles]
    cells = [[((box[k] + box[k + 2]) // (2 * CELL)).astype(F32) for k in range(2)] for box in boxes]
    for at in range(0, ALL, 16):
        apart = CG + REACH if CG <= at < CG + REACH else (REACH if at >= CG + REACH else 0)
        outer = iota((16, 1), 0) + (at - apart)
        for k, box_cells in enumerate(cells):
            wy_high[k, at : at + 16, :], wy_low[k, at : at + 16, :] = two_parts(gauss(box_cells[1], outer))
        wx[at : at + 16, :] = gauss(cells[1][0], outer)
        if at < SIDE:
            columns = iota((16, 1), 0) + at
            wx_left[at : at + 16, :] = gauss(cells[0][0], columns)
            wx_right[at : at + 16, :] = gauss(cells[2][0], columns if at < CG else columns - SIDE)
    for tile, out in ((left, py_left), (right, py_right)):
        out[...] = overlap(tile[1], tile[3], cells_from(0, CG)).astype(BF16)
    inner_sums(
        [tile[4] for tile in tiles],
        (px_left[...], px[...], px_right[...]),
        (py_left[...], py[...], py_right[...]),
        wy_high,
        wy_low,
        (wx_left, wx, wx_right),
        inner,
    )


def inner_kernel(doses, px_left, px, px_right, py_left, py, py_right, wy_high, wy_low, wx_left, wx, wx_right, inner):
    inner_sums(
        [doses[k] for k in range(3)],
        (px_left[...], px[...], px_right[...]),
        (py_left[...], py[...], py_right[...]),
        wy_high,
        wy_low,
        (wx_left, wx, wx_right),
        inner,
    )


def last_inner_kernel(doses, px_left, px, px_right, py_left, py, py_right, wy_high, wy_low, wx, pairs, inner, forward):
    coarse = jnp.concatenate(
        [
            stacked_dot(px[...].astype(F32) * doses[1], py[...], NT),
            stacked_dot(px_left[CG - REACH :, :].astype(F32) * doses[0], py_left[...], NT),
            stacked_dot(px_right[:REACH, :].astype(F32) * doses[2], py_right[...], NT),
        ],
        axis=0,
    )
    across = weighted(coarse, wy_high[1, :CG, :], wy_low[1, :CG, :])
    inner[...] = jnp.sum(across * wx[...], axis=0, keepdims=True)
    forward[...] = pair_sum(doses[1], pairs)


def pair_sum(dose, pairs):
    columns = as_columns(dose)
    total = jnp.zeros((8, SLOTS), F32)
    for k in range(MAXB):
        total += folded_sum(columns[:, k : k + 1] * pairs[k * BLK : (k + 1) * BLK, :])
    return jnp.sum(total, axis=0, keepdims=True)


def exposed(dose, sens, forward, background):
    live = dose > 0.0
    exposure = sens * (forward + BACK_RATIO * background) / (1.0 + BACK_RATIO)
    return jnp.where(live, dose * TARGET_LEVEL / jnp.where(live, exposure, 1.0), 0.0), jnp.where(live, exposure, 0.0)


def new_doses(got_even, got_odd, doses, sens, forward, inner, wy_high, wy_low, wx):
    outer = outer_rows(got_even[...], got_odd[...])
    outer_t = [jnp.transpose(outer[:, k * CG : (k + 1) * CG]) for k in range(3)]
    result = []
    for k, columns in enumerate(per_tile(*outer_t)):
        across = weighted(columns, wy_high[k, CG:, :], wy_low[k, CG:, :])
        background = inner[k] + jnp.sum(across * wx[k][...], axis=0, keepdims=True)
        result.append(exposed(doses[k], sens[k], forward[k], background)[0])
    return result


def first_update_kernel(
    got_even, got_odd, told, told_even, told_odd, own, left, right, inner, pairs, px_left, px, px_right, py_left, py, py_right,
    wy_high, wy_low, wx_left, wx, wx_right, doses_out, sens_out, told_out, send_even, send_odd,
):
    told_left, told_right = sides(told_even[...], told_odd[...])
    forward, sens = zip((told_left[0], told_left[1]), (told[0], told[1]), (told_right[0], told_right[1]))
    doses = new_doses(got_even, got_odd, (left[4], own[4], right[4]), sens, forward, inner, wy_high, wy_low, (wx_left, wx, wx_right))
    for k in range(3):
        sens_out[k] = sens[k]
        doses_out[k] = doses[k]
    told_out[0] = pair_sum(doses[1], pairs)
    strips(doses, (px_left, px, px_right), (py_left, py, py_right), send_even, send_odd)


def update_kernel(
    got_even, got_odd, told, told_even, told_odd, doses, sens, inner, px_left, px, px_right, py_left, py, py_right,
    wy_high, wy_low, wx_left, wx, wx_right, doses_out, send_even, send_odd,
):
    told_left, told_right = sides(told_even[...], told_odd[...])
    before = [doses[k] for k in range(3)]
    factors = [sens[k] for k in range(3)]
    forward = (told_left[0], told[0], told_right[0])
    after = new_doses(got_even, got_odd, before, factors, forward, inner, wy_high, wy_low, (wx_left, wx, wx_right))
    for k in range(3):
        doses_out[k] = after[k]
    last_strips(after, (px_left, px, px_right), (py_left, py, py_right), send_even, send_odd)


def final_kernel(got_even, got_odd, doses, sens, inner, forward, wy_high, wy_low, wx, dose_out, exposure_out):
    outer = outer_rows(got_even[...], got_odd[...])
    columns = jnp.concatenate([jnp.transpose(outer[:, :CG]), jnp.transpose(outer[:, CG:])[: 2 * REACH]], axis=0)
    across = weighted(columns, wy_high[1, CG:, :], wy_low[1, CG:, :])
    background = inner[...] + jnp.sum(across * wx[...], axis=0, keepdims=True)
    dose_out[...], exposure_out[...] = exposed(doses[1], sens[1], forward[...], background)


def shape(*dims, dtype=F32):
    return jax.ShapeDtypeStruct(dims, dtype)


HBM = pl.BlockSpec(memory_space=pltpu.HBM)
VMEM = pl.BlockSpec(memory_space=pltpu.VMEM)


def call(kernel, outs, vmem=24, ins=None, scratch=()):
    extra = {} if ins is None else {"in_specs": ins}
    return pl.pallas_call(
        kernel,
        out_shape=outs,
        scratch_shapes=scratch,
        compiler_params=pltpu.CompilerParams(vmem_limit_bytes=vmem << 20),
        **extra,
    )


def in_hbm(*arrays):
    return [pltpu.with_memory_space_constraint(array, pltpu.HBM) for array in arrays]


def send(value, table):
    return lax.ppermute(value, AXES, table)


def body(shot_boxes, block_counts, tail_shots, doses, pixel_gain):
    row_even, row_odd, col_even, col_odd = pairings()
    row = shape(1, SLOTS)
    rows = shape(3, 1, SLOTS)
    cover = shape(CG, SLOTS, dtype=BF16)
    tile = shape(5, 1, SLOTS)
    weights = shape(3, ALL, SLOTS, dtype=BF16)
    strip = shape(REACH, 3 * CG)
    short = shape(REACH, 2 * CG)
    own = call(
        start_kernel,
        tile,
        ins=[HBM] * 4,
        scratch=(
            pltpu.VMEM((4, 1, SLOTS), jnp.int32),
            pltpu.VMEM((1, NTC), jnp.int32),
            pltpu.VMEM((1, NTC), jnp.int32),
            pltpu.VMEM((1, SLOTS), F32),
            pltpu.SemaphoreType.DMA((4,)),
        ),
    )(*in_hbm(shot_boxes, block_counts, tail_shots, doses))
    far_odd = send(own, col_odd)
    far_even = send(own, col_even)
    px, py, pairs, told = call(
        early_kernel,
        (cover, cover, shape(SLOTS, SLOTS), shape(2, 1, SLOTS)),
        ins=[VMEM, HBM],
        scratch=(
            pltpu.VMEM((TILE, TILE), F32),
            pltpu.VMEM((TILE, 2 * TILE), BF16),
            pltpu.VMEM((TILE, 256), F32),
            pltpu.VMEM((TILE, SLOTS), BF16),
            pltpu.SemaphoreType.DMA,
        ),
    )(own, *in_hbm(pixel_gain))
    told_odd = send(told, col_odd)
    left, right, px_left, px_right, strip_even, strip_odd = call(
        first_strips_kernel, (tile, tile, cover, cover, strip, strip)
    )(own, far_even, far_odd, px, py)
    got_odd = send(strip_odd, row_odd)
    got_even = send(strip_even, row_even)
    told_even = send(told, col_even)
    py_left, py_right, wy_high, wy_low, wx_left, wx, wx_right, inner = call(
        late_kernel, (cover, cover, weights, weights, shape(SIDE, SLOTS), shape(ALL, SLOTS), shape(SIDE, SLOTS), rows)
    )(own, left, right, px_left, px, px_right, py)
    covers = (px_left, px, px_right, py_left, py, py_right)
    weighing = (wy_high, wy_low, wx_left, wx, wx_right)
    doses3, sens, told_next, strip_even, strip_odd = call(first_update_kernel, (rows, rows, shape(1, 1, SLOTS), strip, strip))(
        got_even, got_odd, told, told_even, told_odd, own, left, right, inner, pairs, *covers, *weighing
    )
    told_odd = send(told_next, col_odd)
    got_odd = send(strip_odd, row_odd)
    told_even = send(told_next, col_even)
    got_even = send(strip_even, row_even)
    inner = call(inner_kernel, rows)(doses3, *covers, *weighing)
    doses3, strip_even, strip_odd = call(update_kernel, (rows, short, short))(
        got_even, got_odd, told_next, told_even, told_odd, doses3, sens, inner, *covers, *weighing
    )
    got_odd = send(strip_odd, row_odd)
    got_even = send(strip_even, row_even)
    inner, forward = call(last_inner_kernel, (row, row))(doses3, *covers, wy_high, wy_low, wx, pairs)
    return call(final_kernel, (row, row))(got_even, got_odd, doses3, sens, inner, forward, wy_high, wy_low, wx)


def solution(mesh):
    placed = (P(None, "row", "col"), P("row", None), P("row", None), P("row", "col"), P("row", "col"))
    return jax.shard_map(body, mesh=mesh, in_specs=placed, out_specs=(P("row", "col"), P("row", "col")), check_vma=False)
```

```python
import math

import jax
import jax.numpy as jnp
from jax import lax
from jax.experimental import pallas as pl
from jax.experimental.pallas import tpu as pltpu
from jax.sharding import PartitionSpec as P


TILE = 512
CG = 128
BLK = 128
CELL = 4
BETA = 16
REACH = 32
SLOTS = 1024
NTR = 8
NTC = 16
FORWARD_RANGE = 4.0
BACK_RATIO = 0.75
TARGET_LEVEL = 1.0
F32 = jnp.float32
BF16 = jnp.bfloat16
AXES = ("row", "col")
NT = (((1,), (1,)), ((), ()))
MAXB = 8
SIDE = CG + REACH
ALL = CG + 2 * REACH
MARGINS = (3 * REACH + 2 * 8, 2 * REACH + 8)


def pairings():
    def number(r, c):
        return r * NTC + c

    def table(partner):
        return [(number(r, c), number(*partner(r, c))) for r in range(NTR) for c in range(NTC)]

    def odd(i):
        return ((i - 1) ^ 1) + 1

    row_even = table(lambda r, c: (r ^ 1, c))
    row_odd = table(lambda r, c: (r, c ^ 1) if r in (0, NTR - 1) else (odd(r), c))
    col_even = table(lambda r, c: (r, c ^ 1))
    col_odd = table(lambda r, c: (r ^ 1, c) if c in (0, NTC - 1) else (r, odd(c)))
    return row_even, row_odd, col_even, col_odd


def two_parts(value):
    high = value.astype(BF16)
    low = (value - high.astype(F32)).astype(BF16)
    return high, low


def stacked_dot(value, other, dims):
    rows = value.shape[0]
    parts = jnp.concatenate(two_parts(value), axis=0)
    both = lax.dot_general(parts, other, dims, preferred_element_type=F32)
    return both[:rows] + both[rows:]


def weighted(columns, high, low):
    first, second = two_parts(columns)
    return jnp.dot(
        jnp.concatenate([first, first, second], axis=1), jnp.concatenate([high, low, high], axis=0), preferred_element_type=F32
    )


def overlap(low_edge, high_edge, cells):
    begin = cells * CELL
    covered = jnp.minimum(high_edge, begin + CELL) - jnp.maximum(low_edge, begin)
    return jnp.maximum(covered, 0.0) * (1.0 / CELL)


def gauss(cells, places):
    rate = math.sqrt(math.log2(math.e)) / BETA
    level = -math.log2(math.sqrt(math.pi) * BETA)
    scaled = cells * rate - places.astype(F32) * rate
    square = scaled * scaled
    return jnp.where(square <= (rate * (REACH + 0.5)) ** 2, jnp.exp2(level - square), 0.0)


def iota(shape, axis):
    return lax.broadcasted_iota(jnp.int32, shape, axis)


def is_even(axis):
    return lax.rem(lax.axis_index(axis), 2) == 0


def sides(from_even, from_odd):
    col = lax.axis_index("col")
    even = lax.rem(col, 2) == 0
    left = jnp.where(even, from_odd, from_even)
    right = jnp.where(even, from_even, from_odd)
    return jnp.where(col == 0, 0.0, left), jnp.where(col == NTC - 1, 0.0, right)


def outer_rows(from_even, from_odd):
    row = lax.axis_index("row")
    even = lax.rem(row, 2) == 0
    above = jnp.where(even, from_odd, from_even)
    below = jnp.where(even, from_even, from_odd)
    return jnp.concatenate([jnp.where(row == 0, 0.0, above), jnp.where(row == NTR - 1, 0.0, below)], axis=0)


def send_rows(edges, send_even, send_odd):
    even = is_even("row")
    top, bottom = edges[:REACH], edges[REACH:]
    send_even[...] = jnp.where(even, bottom, top)
    send_odd[...] = jnp.where(even, top, bottom)


def boxes_of(tile):
    return [tile[k].astype(jnp.int32) for k in range(4)]


def cells_from(first, count):
    return (iota((count, SLOTS), 0) + first).astype(F32)


def edge_part(py):
    return jnp.concatenate([py[:REACH, :], py[CG - REACH :, :]], axis=0).astype(F32)


def start_kernel(boxes_in, counts_in, tails_in, doses_in, tile, boxes, counts, tails, doses, arrived):
    copies = [
        pltpu.make_async_copy(source, target, arrived.at[k])
        for k, (source, target) in enumerate(((boxes_in, boxes), (counts_in, counts), (tails_in, tails), (doses_in, doses)))
    ]
    for copy in copies:
        copy.start()
    for copy in copies:
        copy.wait()
    col = lax.axis_index("col")
    totals = (counts[...] - 1) * BLK + tails[...]
    total = jnp.sum(jnp.where(iota((1, NTC), 1) == col, totals, 0), axis=1, keepdims=True)
    live = iota((1, SLOTS), 1) < total
    for k in range(4):
        tile[k] = boxes[k].astype(F32)
    tile[4] = jnp.where(live, doses[...], 0.0)


def as_columns(dose):
    return jnp.transpose(jnp.concatenate([dose[:, k * BLK : (k + 1) * BLK] for k in range(MAXB)], axis=0))


def folded_sum(value):
    return jnp.sum(value.reshape(BLK // 8, 8, SLOTS), axis=0)


def early_kernel(tile, gain_in, px_out, py_out, pairs, told, gain, gain_parts, picked, chosen_x, arrived):
    copy = pltpu.make_async_copy(gain_in, gain, arrived)
    copy.start()
    boxes = boxes_of(tile)
    pixel_x = (boxes[0] + boxes[2]) // 2
    pixel_y = (boxes[1] + boxes[3]) // 2
    for at in range(0, TILE, 16):
        chosen_x[at : at + 16, :] = jnp.where(iota((16, SLOTS), 0) + at == pixel_x, 1.0, 0.0).astype(BF16)
    inverse = 1.0 / FORWARD_RANGE
    box = [tile[k] for k in range(4)]
    centre_x = jnp.broadcast_to((box[0] + box[2]) * (0.5 * inverse), (8, SLOTS))
    centre_y = jnp.broadcast_to((box[1] + box[3]) * (0.5 * inverse), (8, SLOTS))
    columns = jnp.concatenate([b * inverse for b in box] + [tile[4], jnp.zeros((3, SLOTS), F32)], axis=0)
    total = jnp.zeros((8, SLOTS), F32)
    for block in range(MAXB):
        at = block * BLK
        if block == 3:
            copy.wait()
            high, low = two_parts(gain[...])
            gain_parts[...] = jnp.concatenate([high, low], axis=1)
        if block >= 3 and block < 7:
            lanes = slice((block - 3) * 256, (block - 2) * 256)
            chosen = chosen_x[:, lanes]
            picked[...] = jnp.dot(gain_parts[...], jnp.concatenate([chosen, chosen], axis=0), preferred_element_type=F32)
        side = jnp.transpose(columns[:, at : at + BLK])
        for down in range(0, BLK, 8):
            low_x, low_y, high_x, high_y, dose = [side[down : down + 8, k : k + 1] for k in range(5)]
            along_x = lax.erf(centre_x - low_x) - lax.erf(centre_x - high_x)
            along_y = lax.erf(centre_y - low_y) - lax.erf(centre_y - high_y)
            values = (0.25 * along_x) * along_y
            pairs[at + down : at + down + 8, :] = values
            total += dose * values
        if block >= 3 and block < 7:
            found = jnp.zeros((8, 256), F32)
            for row in range(0, TILE, 8):
                found += jnp.where(iota((8, 256), 0) + row == pixel_y[:, lanes], picked[row : row + 8, :], 0.0)
            told[1, :, lanes] = jnp.sum(found, axis=0, keepdims=True)
        if block < 3:
            for first in range(block * 48, min(block * 48 + 48, CG), 16):
                px_out[first : first + 16, :] = overlap(box[0], box[2], cells_from(first, 16)).astype(BF16)
                py_out[first : first + 16, :] = overlap(box[1], box[3], cells_from(first, 16)).astype(BF16)
    told[0] = jnp.sum(total, axis=0, keepdims=True)


def first_strips_kernel(own, got_even, got_odd, px, py, left_out, right_out, px_left, px_right, send_even, send_odd):
    left, right = sides(got_even[...], got_odd[...])
    left_out[...] = left
    right_out[...] = right
    edge_cells = jnp.concatenate([cells_from(0, REACH), cells_from(CG - REACH, REACH)], axis=0)
    edges = [stacked_dot(edge_part(py) * own[4], px[...], NT)]
    for tile, px_out in ((left, px_left), (right, px_right)):
        across = overlap(tile[0], tile[2], cells_from(0, CG)).astype(BF16)
        px_out[...] = across
        edges.append(stacked_dot(overlap(tile[1], tile[3], edge_cells) * tile[4], across, NT))
    send_rows(jnp.concatenate([edges[1], edges[0], edges[2]], axis=1), send_even, send_odd)


def strips(doses, px, py, send_even, send_odd):
    edges = [stacked_dot(edge_part(down) * dose, across[...], NT) for dose, across, down in zip(doses, px, py)]
    send_rows(jnp.concatenate(edges, axis=1), send_even, send_odd)


def last_strips(doses, px, py, send_even, send_odd):
    edges = [
        stacked_dot(edge_part(py[1]) * doses[1], px[1][...], NT),
        stacked_dot(edge_part(py[0]) * doses[0], px[0][CG - REACH :, :], NT),
        stacked_dot(edge_part(py[2]) * doses[2], px[2][:REACH, :], NT),
        jnp.zeros((2 * REACH, 2 * CG - ALL), F32),
    ]
    send_rows(jnp.concatenate(edges, axis=1), send_even, send_odd)


def per_tile(left, own, right, margin):
    return (
        jnp.concatenate([left[CG - margin :], own[:REACH]], axis=0),
        jnp.concatenate([own, left[CG - REACH :], right[:REACH]], axis=0),
        jnp.concatenate([right[:margin], own[CG - REACH :]], axis=0),
    )


def weights_along(wx, margin):
    left, own, right = wx
    return left[CG - margin :, :], own[...], jnp.concatenate([right[:margin, :], right[CG:, :]], axis=0)


def inner_sums(doses, px, py, wy_high, wy_low, wx, inner, margin):
    coarse = [stacked_dot(across.astype(F32) * dose, down, NT) for dose, across, down in zip(doses, px, py)]
    for k, (columns, along) in enumerate(zip(per_tile(*coarse, margin), weights_along(wx, margin))):
        across = weighted(columns, wy_high[k, :CG, :], wy_low[k, :CG, :])
        inner[k] = jnp.sum(across * along, axis=0, keepdims=True)


def late_kernel(own, left, right, px_left, px, px_right, py, py_left, py_right, wy_high, wy_low, wx_left, wx, wx_right, inner):
    tiles = (left, own, right)
    boxes = [boxes_of(tile) for tile in tiles]
    cells = [[((box[k] + box[k + 2]) // (2 * CELL)).astype(F32) for k in range(2)] for box in boxes]
    for at in range(0, ALL, 16):
        apart = CG + REACH if CG <= at < CG + REACH else (REACH if at >= CG + REACH else 0)
        outer = iota((16, 1), 0) + (at - apart)
        for k, box_cells in enumerate(cells):
            wy_high[k, at : at + 16, :], wy_low[k, at : at + 16, :] = two_parts(gauss(box_cells[1], outer))
        wx[at : at + 16, :] = gauss(cells[1][0], outer)
        if at < SIDE:
            columns = iota((16, 1), 0) + at
            wx_left[at : at + 16, :] = gauss(cells[0][0], columns)
            wx_right[at : at + 16, :] = gauss(cells[2][0], columns if at < CG else columns - SIDE)
    for tile, out in ((left, py_left), (right, py_right)):
        out[...] = overlap(tile[1], tile[3], cells_from(0, CG)).astype(BF16)
    inner_sums(
        [tile[4] for tile in tiles],
        (px_left[...], px[...], px_right[...]),
        (py_left[...], py[...], py_right[...]),
        wy_high,
        wy_low,
        (wx_left, wx, wx_right),
        inner,
        MARGINS[0],
    )


def inner_kernel(doses, px_left, px, px_right, py_left, py, py_right, wy_high, wy_low, wx_left, wx, wx_right, inner):
    inner_sums(
        [doses[k] for k in range(3)],
        (px_left[...], px[...], px_right[...]),
        (py_left[...], py[...], py_right[...]),
        wy_high,
        wy_low,
        (wx_left, wx, wx_right),
        inner,
        MARGINS[1],
    )


def last_inner_kernel(doses, px_left, px, px_right, py_left, py, py_right, wy_high, wy_low, wx, pairs, inner, forward):
    coarse = jnp.concatenate(
        [
            stacked_dot(px[...].astype(F32) * doses[1], py[...], NT),
            stacked_dot(px_left[CG - REACH :, :].astype(F32) * doses[0], py_left[...], NT),
            stacked_dot(px_right[:REACH, :].astype(F32) * doses[2], py_right[...], NT),
        ],
        axis=0,
    )
    across = weighted(coarse, wy_high[1, :CG, :], wy_low[1, :CG, :])
    inner[...] = jnp.sum(across * wx[...], axis=0, keepdims=True)
    forward[...] = pair_sum(doses[1], pairs)


def pair_sum(dose, pairs):
    columns = as_columns(dose)
    total = jnp.zeros((8, SLOTS), F32)
    for k in range(MAXB):
        total += folded_sum(columns[:, k : k + 1] * pairs[k * BLK : (k + 1) * BLK, :])
    return jnp.sum(total, axis=0, keepdims=True)


def exposed(dose, sens, forward, background):
    live = dose > 0.0
    exposure = sens * (forward + BACK_RATIO * background) / (1.0 + BACK_RATIO)
    return jnp.where(live, dose * TARGET_LEVEL / jnp.where(live, exposure, 1.0), 0.0), jnp.where(live, exposure, 0.0)


def new_doses(got_even, got_odd, doses, sens, forward, inner, wy_high, wy_low, wx, margin):
    outer = outer_rows(got_even[...], got_odd[...])
    outer_t = [jnp.transpose(outer[:, k * CG : (k + 1) * CG]) for k in range(3)]
    result = []
    for k, (columns, along) in enumerate(zip(per_tile(*outer_t, margin), weights_along(wx, margin))):
        across = weighted(columns, wy_high[k, CG:, :], wy_low[k, CG:, :])
        background = inner[k] + jnp.sum(across * along, axis=0, keepdims=True)
        result.append(exposed(doses[k], sens[k], forward[k], background)[0])
    return result


def first_update_kernel(
    got_even, got_odd, told, told_even, told_odd, own, left, right, inner, pairs, px_left, px, px_right, py_left, py, py_right,
    wy_high, wy_low, wx_left, wx, wx_right, doses_out, sens_out, told_out, send_even, send_odd,
):
    told_left, told_right = sides(told_even[...], told_odd[...])
    forward, sens = zip((told_left[0], told_left[1]), (told[0], told[1]), (told_right[0], told_right[1]))
    doses = new_doses(got_even, got_odd, (left[4], own[4], right[4]), sens, forward, inner, wy_high, wy_low, (wx_left, wx, wx_right), MARGINS[0])
    for k in range(3):
        sens_out[k] = sens[k]
        doses_out[k] = doses[k]
    told_out[0] = pair_sum(doses[1], pairs)
    strips(doses, (px_left, px, px_right), (py_left, py, py_right), send_even, send_odd)


def update_kernel(
    got_even, got_odd, told, told_even, told_odd, doses, sens, inner, px_left, px, px_right, py_left, py, py_right,
    wy_high, wy_low, wx_left, wx, wx_right, doses_out, send_even, send_odd,
):
    told_left, told_right = sides(told_even[...], told_odd[...])
    before = [doses[k] for k in range(3)]
    factors = [sens[k] for k in range(3)]
    forward = (told_left[0], told[0], told_right[0])
    after = new_doses(got_even, got_odd, before, factors, forward, inner, wy_high, wy_low, (wx_left, wx, wx_right), MARGINS[1])
    for k in range(3):
        doses_out[k] = after[k]
    last_strips(after, (px_left, px, px_right), (py_left, py, py_right), send_even, send_odd)


def final_kernel(got_even, got_odd, doses, sens, inner, forward, wy_high, wy_low, wx, dose_out, exposure_out):
    outer = outer_rows(got_even[...], got_odd[...])
    columns = jnp.concatenate([jnp.transpose(outer[:, :CG]), jnp.transpose(outer[:, CG:])[: 2 * REACH]], axis=0)
    across = weighted(columns, wy_high[1, CG:, :], wy_low[1, CG:, :])
    background = inner[...] + jnp.sum(across * wx[...], axis=0, keepdims=True)
    dose_out[...], exposure_out[...] = exposed(doses[1], sens[1], forward[...], background)


def shape(*dims, dtype=F32):
    return jax.ShapeDtypeStruct(dims, dtype)


HBM = pl.BlockSpec(memory_space=pltpu.HBM)
VMEM = pl.BlockSpec(memory_space=pltpu.VMEM)


def call(kernel, outs, vmem=24, ins=None, scratch=()):
    extra = {} if ins is None else {"in_specs": ins}
    return pl.pallas_call(
        kernel,
        out_shape=outs,
        scratch_shapes=scratch,
        compiler_params=pltpu.CompilerParams(vmem_limit_bytes=vmem << 20),
        **extra,
    )


def in_hbm(*arrays):
    return [pltpu.with_memory_space_constraint(array, pltpu.HBM) for array in arrays]


def send(value, table):
    return lax.ppermute(value, AXES, table)


def body(shot_boxes, block_counts, tail_shots, doses, pixel_gain):
    row_even, row_odd, col_even, col_odd = pairings()
    row = shape(1, SLOTS)
    rows = shape(3, 1, SLOTS)
    cover = shape(CG, SLOTS, dtype=BF16)
    tile = shape(5, 1, SLOTS)
    weights = shape(3, ALL, SLOTS, dtype=BF16)
    strip = shape(REACH, 3 * CG)
    short = shape(REACH, 2 * CG)
    own = call(
        start_kernel,
        tile,
        ins=[HBM] * 4,
        scratch=(
            pltpu.VMEM((4, 1, SLOTS), jnp.int32),
            pltpu.VMEM((1, NTC), jnp.int32),
            pltpu.VMEM((1, NTC), jnp.int32),
            pltpu.VMEM((1, SLOTS), F32),
            pltpu.SemaphoreType.DMA((4,)),
        ),
    )(*in_hbm(shot_boxes, block_counts, tail_shots, doses))
    far_odd = send(own, col_odd)
    far_even = send(own, col_even)
    px, py, pairs, told = call(
        early_kernel,
        (cover, cover, shape(SLOTS, SLOTS), shape(2, 1, SLOTS)),
        ins=[VMEM, HBM],
        scratch=(
            pltpu.VMEM((TILE, TILE), F32),
            pltpu.VMEM((TILE, 2 * TILE), BF16),
            pltpu.VMEM((TILE, 256), F32),
            pltpu.VMEM((TILE, SLOTS), BF16),
            pltpu.SemaphoreType.DMA,
        ),
    )(own, *in_hbm(pixel_gain))
    told_odd = send(told, col_odd)
    left, right, px_left, px_right, strip_even, strip_odd = call(
        first_strips_kernel, (tile, tile, cover, cover, strip, strip)
    )(own, far_even, far_odd, px, py)
    got_odd = send(strip_odd, row_odd)
    got_even = send(strip_even, row_even)
    told_even = send(told, col_even)
    py_left, py_right, wy_high, wy_low, wx_left, wx, wx_right, inner = call(
        late_kernel, (cover, cover, weights, weights, shape(SIDE, SLOTS), shape(ALL, SLOTS), shape(SIDE, SLOTS), rows)
    )(own, left, right, px_left, px, px_right, py)
    covers = (px_left, px, px_right, py_left, py, py_right)
    weighing = (wy_high, wy_low, wx_left, wx, wx_right)
    doses3, sens, told_next, strip_even, strip_odd = call(first_update_kernel, (rows, rows, shape(1, 1, SLOTS), strip, strip))(
        got_even, got_odd, told, told_even, told_odd, own, left, right, inner, pairs, *covers, *weighing
    )
    told_odd = send(told_next, col_odd)
    got_odd = send(strip_odd, row_odd)
    told_even = send(told_next, col_even)
    got_even = send(strip_even, row_even)
    inner = call(inner_kernel, rows)(doses3, *covers, *weighing)
    doses3, strip_even, strip_odd = call(update_kernel, (rows, short, short))(
        got_even, got_odd, told_next, told_even, told_odd, doses3, sens, inner, *covers, *weighing
    )
    got_odd = send(strip_odd, row_odd)
    got_even = send(strip_even, row_even)
    inner, forward = call(last_inner_kernel, (row, row))(doses3, *covers, wy_high, wy_low, wx, pairs)
    return call(final_kernel, (row, row))(got_even, got_odd, doses3, sens, inner, forward, wy_high, wy_low, wx)


def solution(mesh):
    placed = (P(None, "row", "col"), P("row", None), P("row", None), P("row", "col"), P("row", "col"))
    return jax.shard_map(body, mesh=mesh, in_specs=placed, out_specs=(P("row", "col"), P("row", "col")), check_vma=False)
```

```python
import math

import jax
import jax.numpy as jnp
from jax import lax
from jax.experimental import pallas as pl
from jax.experimental.pallas import tpu as pltpu
from jax.sharding import PartitionSpec as P


TILE = 512
CG = 128
BLK = 128
CELL = 4
BETA = 16
REACH = 32
SLOTS = 1024
NTR = 8
NTC = 16
FORWARD_RANGE = 4.0
BACK_RATIO = 0.75
TARGET_LEVEL = 1.0
F32 = jnp.float32
BF16 = jnp.bfloat16
AXES = ("row", "col")
NT = (((1,), (1,)), ((), ()))
MAXB = 8
SIDE = CG + REACH
ALL = CG + 2 * REACH
MARGINS = (3 * REACH + 2 * 8, 2 * REACH + 8)


def pairings():
    def number(r, c):
        return r * NTC + c

    def table(partner):
        return [(number(r, c), number(*partner(r, c))) for r in range(NTR) for c in range(NTC)]

    def odd(i):
        return ((i - 1) ^ 1) + 1

    row_even = table(lambda r, c: (r ^ 1, c))
    row_odd = table(lambda r, c: (r, c ^ 1) if r in (0, NTR - 1) else (odd(r), c))
    col_even = table(lambda r, c: (r, c ^ 1))
    col_odd = table(lambda r, c: (r ^ 1, c) if c in (0, NTC - 1) else (r, odd(c)))
    return row_even, row_odd, col_even, col_odd


def two_parts(value):
    high = value.astype(BF16)
    low = (value - high.astype(F32)).astype(BF16)
    return high, low


def stacked_dot(value, other, dims):
    rows = value.shape[0]
    parts = jnp.concatenate(two_parts(value), axis=0)
    both = lax.dot_general(parts, other, dims, preferred_element_type=F32)
    return both[:rows] + both[rows:]


def weighted(columns, high, low):
    first, second = two_parts(columns)
    return jnp.dot(
        jnp.concatenate([first, first, second], axis=1), jnp.concatenate([high, low, high], axis=0), preferred_element_type=F32
    )


def overlap(low_edge, high_edge, cells):
    begin = cells * CELL
    covered = jnp.minimum(high_edge, begin + CELL) - jnp.maximum(low_edge, begin)
    return jnp.maximum(covered, 0.0) * (1.0 / CELL)


def gauss(cells, places):
    rate = math.sqrt(math.log2(math.e)) / BETA
    level = -math.log2(math.sqrt(math.pi) * BETA)
    scaled = cells * rate - places.astype(F32) * rate
    square = scaled * scaled
    return jnp.where(square <= (rate * (REACH + 0.5)) ** 2, jnp.exp2(level - square), 0.0)


def iota(shape, axis):
    return lax.broadcasted_iota(jnp.int32, shape, axis)


def is_even(axis):
    return lax.rem(lax.axis_index(axis), 2) == 0


def sides(from_even, from_odd):
    col = lax.axis_index("col")
    even = lax.rem(col, 2) == 0
    left = jnp.where(even, from_odd, from_even)
    right = jnp.where(even, from_even, from_odd)
    return jnp.where(col == 0, 0.0, left), jnp.where(col == NTC - 1, 0.0, right)


def outer_rows(from_even, from_odd):
    row = lax.axis_index("row")
    even = lax.rem(row, 2) == 0
    above = jnp.where(even, from_odd, from_even)
    below = jnp.where(even, from_even, from_odd)
    return jnp.concatenate([jnp.where(row == 0, 0.0, above), jnp.where(row == NTR - 1, 0.0, below)], axis=0)


def send_rows(edges, send_even, send_odd):
    even = is_even("row")
    top, bottom = edges[:REACH], edges[REACH:]
    send_even[...] = jnp.where(even, bottom, top)
    send_odd[...] = jnp.where(even, top, bottom)


def boxes_of(tile):
    return [tile[k].astype(jnp.int32) for k in range(4)]


def cells_from(first, count):
    return (iota((count, SLOTS), 0) + first).astype(F32)


def edge_part(py):
    return jnp.concatenate([py[:REACH, :], py[CG - REACH :, :]], axis=0).astype(F32)


def start_kernel(boxes_in, counts_in, tails_in, doses_in, tile, boxes, counts, tails, doses, arrived):
    copies = [
        pltpu.make_async_copy(source, target, arrived.at[k])
        for k, (source, target) in enumerate(((boxes_in, boxes), (counts_in, counts), (tails_in, tails), (doses_in, doses)))
    ]
    for copy in copies:
        copy.start()
    for copy in copies:
        copy.wait()
    col = lax.axis_index("col")
    totals = (counts[...] - 1) * BLK + tails[...]
    total = jnp.sum(jnp.where(iota((1, NTC), 1) == col, totals, 0), axis=1, keepdims=True)
    live = iota((1, SLOTS), 1) < total
    for k in range(4):
        tile[k] = boxes[k].astype(F32)
    tile[4] = jnp.where(live, doses[...], 0.0)


def as_columns(dose):
    return jnp.transpose(jnp.concatenate([dose[:, k * BLK : (k + 1) * BLK] for k in range(MAXB)], axis=0))


def folded_sum(value):
    return jnp.sum(value.reshape(BLK // 8, 8, SLOTS), axis=0)


def early_kernel(tile, gain_in, px_out, py_out, pairs, told, gain, gain_parts, picked, chosen_x, arrived):
    copy = pltpu.make_async_copy(gain_in, gain, arrived)
    copy.start()
    boxes = boxes_of(tile)
    pixel_x = (boxes[0] + boxes[2]) // 2
    pixel_y = (boxes[1] + boxes[3]) // 2
    for at in range(0, TILE, 16):
        chosen_x[at : at + 16, :] = jnp.where(iota((16, SLOTS), 0) + at == pixel_x, 1.0, 0.0).astype(BF16)
    inverse = 1.0 / FORWARD_RANGE
    box = [tile[k] for k in range(4)]
    centre_x = jnp.broadcast_to((box[0] + box[2]) * (0.5 * inverse), (8, SLOTS))
    centre_y = jnp.broadcast_to((box[1] + box[3]) * (0.5 * inverse), (8, SLOTS))
    columns = jnp.concatenate([b * inverse for b in box] + [tile[4], jnp.zeros((3, SLOTS), F32)], axis=0)
    total = jnp.zeros((8, SLOTS), F32)
    for block in range(MAXB):
        at = block * BLK
        if block == 3:
            copy.wait()
            high, low = two_parts(gain[...])
            gain_parts[...] = jnp.concatenate([high, low], axis=1)
        if block >= 3 and block < 7:
            lanes = slice((block - 3) * 256, (block - 2) * 256)
            chosen = chosen_x[:, lanes]
            picked[...] = jnp.dot(gain_parts[...], jnp.concatenate([chosen, chosen], axis=0), preferred_element_type=F32)
        side = jnp.transpose(columns[:, at : at + BLK])
        for down in range(0, BLK, 8):
            low_x, low_y, high_x, high_y, dose = [side[down : down + 8, k : k + 1] for k in range(5)]
            along_x = lax.erf(centre_x - low_x) - lax.erf(centre_x - high_x)
            along_y = lax.erf(centre_y - low_y) - lax.erf(centre_y - high_y)
            values = (0.25 * along_x) * along_y
            pairs[at + down : at + down + 8, :] = values
            total += dose * values
        if block >= 3 and block < 7:
            found = jnp.zeros((8, 256), F32)
            for row in range(0, TILE, 8):
                found += jnp.where(iota((8, 256), 0) + row == pixel_y[:, lanes], picked[row : row + 8, :], 0.0)
            told[1, :, lanes] = jnp.sum(found, axis=0, keepdims=True)
        if block < 3:
            for first in range(block * 48, min(block * 48 + 48, CG), 16):
                px_out[first : first + 16, :] = overlap(box[0], box[2], cells_from(first, 16)).astype(BF16)
                py_out[first : first + 16, :] = overlap(box[1], box[3], cells_from(first, 16)).astype(BF16)
    told[0] = jnp.sum(total, axis=0, keepdims=True)


def first_strips_kernel(own, got_even, got_odd, px, py, left_out, right_out, px_left, px_right, send_even, send_odd):
    left, right = sides(got_even[...], got_odd[...])
    left_out[...] = left
    right_out[...] = right
    edge_cells = jnp.concatenate([cells_from(0, REACH), cells_from(CG - REACH, REACH)], axis=0)
    edges = [stacked_dot(edge_part(py) * own[4], px[...], NT)]
    for tile, px_out in ((left, px_left), (right, px_right)):
        across = overlap(tile[0], tile[2], cells_from(0, CG)).astype(BF16)
        px_out[...] = across
        edges.append(stacked_dot(overlap(tile[1], tile[3], edge_cells) * tile[4], across, NT))
    send_rows(jnp.concatenate([edges[1], edges[0], edges[2]], axis=1), send_even, send_odd)


def strips(doses, px, py, send_even, send_odd):
    edges = [stacked_dot(edge_part(down) * dose, across[...], NT) for dose, across, down in zip(doses, px, py)]
    send_rows(jnp.concatenate(edges, axis=1), send_even, send_odd)


def last_strips(doses, px, py, send_even, send_odd):
    edges = [
        stacked_dot(edge_part(py[1]) * doses[1], px[1][...], NT),
        stacked_dot(edge_part(py[0]) * doses[0], px[0][CG - REACH :, :], NT),
        stacked_dot(edge_part(py[2]) * doses[2], px[2][:REACH, :], NT),
        jnp.zeros((2 * REACH, 2 * CG - ALL), F32),
    ]
    send_rows(jnp.concatenate(edges, axis=1), send_even, send_odd)


def per_tile(left, own, right, margin):
    return (
        jnp.concatenate([left[CG - margin :], own[:REACH]], axis=0),
        jnp.concatenate([own, left[CG - REACH :], right[:REACH]], axis=0),
        jnp.concatenate([right[:margin], own[CG - REACH :]], axis=0),
    )


def weights_along(wx, margin):
    left, own, right = wx
    return left[CG - margin :, :], own[...], jnp.concatenate([right[:margin, :], right[CG:, :]], axis=0)


def inner_sums(doses, px, py, wy_high, wy_low, wx, inner, margin):
    coarse = [stacked_dot(across.astype(F32) * dose, down, NT) for dose, across, down in zip(doses, px, py)]
    for k, (columns, along) in enumerate(zip(per_tile(*coarse, margin), weights_along(wx, margin))):
        across = weighted(columns, wy_high[k, :CG, :], wy_low[k, :CG, :])
        inner[k] = jnp.sum(across * along, axis=0, keepdims=True)


def late_kernel(own, left, right, px_left, px, px_right, py, py_left, py_right, wy_high, wy_low, wx_left, wx, wx_right, inner):
    tiles = (left, own, right)
    boxes = [boxes_of(tile) for tile in tiles]
    cells = [[((box[k] + box[k + 2]) // (2 * CELL)).astype(F32) for k in range(2)] for box in boxes]
    for at in range(0, ALL, 16):
        apart = CG + REACH if CG <= at < CG + REACH else (REACH if at >= CG + REACH else 0)
        outer = iota((16, 1), 0) + (at - apart)
        for k, box_cells in enumerate(cells):
            wy_high[k, at : at + 16, :], wy_low[k, at : at + 16, :] = two_parts(gauss(box_cells[1], outer))
        wx[at : at + 16, :] = gauss(cells[1][0], outer)
        if at < SIDE:
            columns = iota((16, 1), 0) + at
            wx_left[at : at + 16, :] = gauss(cells[0][0], columns)
            wx_right[at : at + 16, :] = gauss(cells[2][0], columns if at < CG else columns - SIDE)
    for tile, out in ((left, py_left), (right, py_right)):
        out[...] = overlap(tile[1], tile[3], cells_from(0, CG)).astype(BF16)
    inner_sums(
        [tile[4] for tile in tiles],
        (px_left[...], px[...], px_right[...]),
        (py_left[...], py[...], py_right[...]),
        wy_high,
        wy_low,
        (wx_left, wx, wx_right),
        inner,
        MARGINS[0],
    )


def inner_kernel(doses, px_left, px, px_right, py_left, py, py_right, wy_high, wy_low, wx_left, wx, wx_right, inner):
    inner_sums(
        [doses[k] for k in range(3)],
        (px_left[...], px[...], px_right[...]),
        (py_left[...], py[...], py_right[...]),
        wy_high,
        wy_low,
        (wx_left, wx, wx_right),
        inner,
        MARGINS[1],
    )


def last_inner_kernel(doses, px_left, px, px_right, py_left, py, py_right, wy_high, wy_low, wx, pairs, inner, forward):
    coarse = jnp.concatenate(
        [
            stacked_dot(px[...].astype(F32) * doses[1], py[...], NT),
            stacked_dot(px_left[CG - REACH :, :].astype(F32) * doses[0], py_left[...], NT),
            stacked_dot(px_right[:REACH, :].astype(F32) * doses[2], py_right[...], NT),
        ],
        axis=0,
    )
    across = weighted(coarse, wy_high[1, :CG, :], wy_low[1, :CG, :])
    inner[...] = jnp.sum(across * wx[...], axis=0, keepdims=True)
    forward[...] = pair_sum(doses[1], pairs)


def pair_sum(dose, pairs):
    columns = as_columns(dose)
    total = jnp.zeros((8, SLOTS), F32)
    for k in range(MAXB):
        total += folded_sum(columns[:, k : k + 1] * pairs[k * BLK : (k + 1) * BLK, :])
    return jnp.sum(total, axis=0, keepdims=True)


def exposed(dose, sens, forward, background):
    live = dose > 0.0
    exposure = sens * (forward + BACK_RATIO * background) / (1.0 + BACK_RATIO)
    return jnp.where(live, dose * TARGET_LEVEL / jnp.where(live, exposure, 1.0), 0.0), jnp.where(live, exposure, 0.0)


def new_doses(got_even, got_odd, doses, sens, forward, inner, wy_high, wy_low, wx, margin):
    outer = outer_rows(got_even[...], got_odd[...])
    outer_t = [jnp.transpose(outer[:, k * CG : (k + 1) * CG]) for k in range(3)]
    result = []
    for k, (columns, along) in enumerate(zip(per_tile(*outer_t, margin), weights_along(wx, margin))):
        across = weighted(columns, wy_high[k, CG:, :], wy_low[k, CG:, :])
        background = inner[k] + jnp.sum(across * along, axis=0, keepdims=True)
        result.append(exposed(doses[k], sens[k], forward[k], background)[0])
    return result


def first_update_kernel(
    got_even, got_odd, told, told_even, told_odd, own, left, right, inner, pairs, px_left, px, px_right, py_left, py, py_right,
    wy_high, wy_low, wx_left, wx, wx_right, doses_out, sens_out, told_out, send_even, send_odd,
):
    told_left, told_right = sides(told_even[...], told_odd[...])
    forward, sens = zip((told_left[0], told_left[1]), (told[0], told[1]), (told_right[0], told_right[1]))
    doses = new_doses(got_even, got_odd, (left[4], own[4], right[4]), sens, forward, inner, wy_high, wy_low, (wx_left, wx, wx_right), MARGINS[0])
    for k in range(3):
        sens_out[k] = sens[k]
        doses_out[k] = doses[k]
    told_out[0] = pair_sum(doses[1], pairs)
    strips(doses, (px_left, px, px_right), (py_left, py, py_right), send_even, send_odd)


def update_kernel(
    got_even, got_odd, told, told_even, told_odd, doses, sens, inner, px_left, px, px_right, py_left, py, py_right,
    wy_high, wy_low, wx_left, wx, wx_right, doses_out, send_even, send_odd,
):
    told_left, told_right = sides(told_even[...], told_odd[...])
    before = [doses[k] for k in range(3)]
    factors = [sens[k] for k in range(3)]
    forward = (told_left[0], told[0], told_right[0])
    after = new_doses(got_even, got_odd, before, factors, forward, inner, wy_high, wy_low, (wx_left, wx, wx_right), MARGINS[1])
    for k in range(3):
        doses_out[k] = after[k]
    last_strips(after, (px_left, px, px_right), (py_left, py, py_right), send_even, send_odd)


def last_result(got_even, got_odd, doses, sens, inner, forward, wy_high, wy_low, wx, results):
    dose_out, exposure_out, dose, exposure, sent = results
    outer = outer_rows(got_even[...], got_odd[...])
    columns = jnp.concatenate([jnp.transpose(outer[:, :CG]), jnp.transpose(outer[:, CG:])[: 2 * REACH]], axis=0)
    across = weighted(columns, wy_high[1, CG:, :], wy_low[1, CG:, :])
    background = inner[...] + jnp.sum(across * wx[...], axis=0, keepdims=True)
    dose[...], exposure[...] = exposed(doses[1], sens[1], forward[...], background)
    copies = [pltpu.make_async_copy(dose, dose_out, sent.at[0]), pltpu.make_async_copy(exposure, exposure_out, sent.at[1])]
    for copy in copies:
        copy.start()
    for copy in copies:
        copy.wait()


def at_window_edge():
    row = lax.axis_index("row")
    return (row == 0) | (row == NTR - 1)


def edge_kernel(got_even, doses, sens, inner, forward, wy_high, wy_low, wx, *results):
    @pl.when(at_window_edge())
    def _():
        last_result(got_even, got_even, doses, sens, inner, forward, wy_high, wy_low, wx, results)


def final_kernel(got_even, got_odd, doses, sens, inner, forward, wy_high, wy_low, wx, edge_dose, edge_exposure, *results):
    @pl.when(jnp.logical_not(at_window_edge()))
    def _():
        last_result(got_even, got_odd, doses, sens, inner, forward, wy_high, wy_low, wx, results)


def shape(*dims, dtype=F32):
    return jax.ShapeDtypeStruct(dims, dtype)


HBM = pl.BlockSpec(memory_space=pltpu.HBM)
VMEM = pl.BlockSpec(memory_space=pltpu.VMEM)


def call(kernel, outs, vmem=24, ins=None, scratch=(), **extra):
    if ins is not None:
        extra["in_specs"] = ins
    return pl.pallas_call(
        kernel,
        out_shape=outs,
        scratch_shapes=scratch,
        compiler_params=pltpu.CompilerParams(vmem_limit_bytes=vmem << 20),
        **extra,
    )


def in_hbm(*arrays):
    return [pltpu.with_memory_space_constraint(array, pltpu.HBM) for array in arrays]


def send(value, table):
    return lax.ppermute(value, AXES, table)


def body(shot_boxes, block_counts, tail_shots, doses, pixel_gain):
    row_even, row_odd, col_even, col_odd = pairings()
    row = shape(1, SLOTS)
    rows = shape(3, 1, SLOTS)
    cover = shape(CG, SLOTS, dtype=BF16)
    tile = shape(5, 1, SLOTS)
    weights = shape(3, ALL, SLOTS, dtype=BF16)
    strip = shape(REACH, 3 * CG)
    short = shape(REACH, 2 * CG)
    own = call(
        start_kernel,
        tile,
        ins=[HBM] * 4,
        scratch=(
            pltpu.VMEM((4, 1, SLOTS), jnp.int32),
            pltpu.VMEM((1, NTC), jnp.int32),
            pltpu.VMEM((1, NTC), jnp.int32),
            pltpu.VMEM((1, SLOTS), F32),
            pltpu.SemaphoreType.DMA((4,)),
        ),
    )(*in_hbm(shot_boxes, block_counts, tail_shots, doses))
    far_odd = send(own, col_odd)
    far_even = send(own, col_even)
    px, py, pairs, told = call(
        early_kernel,
        (cover, cover, shape(SLOTS, SLOTS), shape(2, 1, SLOTS)),
        ins=[VMEM, HBM],
        scratch=(
            pltpu.VMEM((TILE, TILE), F32),
            pltpu.VMEM((TILE, 2 * TILE), BF16),
            pltpu.VMEM((TILE, 256), F32),
            pltpu.VMEM((TILE, SLOTS), BF16),
            pltpu.SemaphoreType.DMA,
        ),
    )(own, *in_hbm(pixel_gain))
    told_odd = send(told, col_odd)
    left, right, px_left, px_right, strip_even, strip_odd = call(
        first_strips_kernel, (tile, tile, cover, cover, strip, strip)
    )(own, far_even, far_odd, px, py)
    got_odd = send(strip_odd, row_odd)
    got_even = send(strip_even, row_even)
    told_even = send(told, col_even)
    py_left, py_right, wy_high, wy_low, wx_left, wx, wx_right, inner = call(
        late_kernel, (cover, cover, weights, weights, shape(SIDE, SLOTS), shape(ALL, SLOTS), shape(SIDE, SLOTS), rows)
    )(own, left, right, px_left, px, px_right, py)
    covers = (px_left, px, px_right, py_left, py, py_right)
    weighing = (wy_high, wy_low, wx_left, wx, wx_right)
    doses3, sens, told_next, strip_even, strip_odd = call(first_update_kernel, (rows, rows, shape(1, 1, SLOTS), strip, strip))(
        got_even, got_odd, told, told_even, told_odd, own, left, right, inner, pairs, *covers, *weighing
    )
    told_odd = send(told_next, col_odd)
    got_odd = send(strip_odd, row_odd)
    told_even = send(told_next, col_even)
    got_even = send(strip_even, row_even)
    inner = call(inner_kernel, rows)(doses3, *covers, *weighing)
    doses3, strip_even, strip_odd = call(update_kernel, (rows, short, short))(
        got_even, got_odd, told_next, told_even, told_odd, doses3, sens, inner, *covers, *weighing
    )
    got_odd = send(strip_odd, row_odd)
    got_even = send(strip_even, row_even)
    inner, forward = call(last_inner_kernel, (row, row))(doses3, *covers, wy_high, wy_low, wx, pairs)
    results = {
        "out_specs": (HBM, HBM),
        "scratch": (pltpu.VMEM((1, SLOTS), F32), pltpu.VMEM((1, SLOTS), F32), pltpu.SemaphoreType.DMA((2,))),
    }
    common = (doses3, sens, inner, forward, wy_high, wy_low, wx)
    edge = call(edge_kernel, (row, row), **results)(got_even, *common)
    return call(final_kernel, (row, row), ins=[VMEM] * 9 + [HBM] * 2, input_output_aliases={9: 0, 10: 1}, **results)(
        got_even, got_odd, *common, *edge
    )


def solution(mesh):
    placed = (P(None, "row", "col"), P("row", None), P("row", None), P("row", "col"), P("row", "col"))
    return jax.shard_map(body, mesh=mesh, in_specs=placed, out_specs=(P("row", "col"), P("row", "col")), check_vma=False)
```

```python
import math

import jax
import jax.numpy as jnp
from jax import lax
from jax.experimental import pallas as pl
from jax.experimental.pallas import tpu as pltpu
from jax.sharding import PartitionSpec as P


TILE = 512
CG = 128
BLK = 128
CELL = 4
BETA = 16
REACH = 32
SLOTS = 1024
NTR = 8
NTC = 16
FORWARD_RANGE = 4.0
BACK_RATIO = 0.75
TARGET_LEVEL = 1.0
F32 = jnp.float32
BF16 = jnp.bfloat16
AXES = ("row", "col")
NT = (((1,), (1,)), ((), ()))
MAXB = 8
SIDE = CG + REACH
PER_CELL = 1.0 / CELL**2
ALL = CG + 2 * REACH
MARGINS = (3 * REACH + 2 * 8, 2 * REACH + 8)


def pairings():
    def number(r, c):
        return r * NTC + c

    def table(partner):
        return [(number(r, c), number(*partner(r, c))) for r in range(NTR) for c in range(NTC)]

    def odd(i):
        return ((i - 1) ^ 1) + 1

    row_even = table(lambda r, c: (r ^ 1, c))
    row_odd = table(lambda r, c: (r, c ^ 1) if r in (0, NTR - 1) else (odd(r), c))
    col_even = table(lambda r, c: (r, c ^ 1))
    col_odd = table(lambda r, c: (r ^ 1, c) if c in (0, NTC - 1) else (r, odd(c)))
    return row_even, row_odd, col_even, col_odd


def two_parts(value):
    high = value.astype(BF16)
    low = (value - high.astype(F32)).astype(BF16)
    return high, low


def stacked_dot(value, other, dims):
    rows = value.shape[0]
    parts = jnp.concatenate(two_parts(value), axis=0)
    both = lax.dot_general(parts, other, dims, preferred_element_type=F32)
    return both[:rows] + both[rows:]


def weighted(columns, high, low):
    first, second = two_parts(columns)
    return jnp.dot(
        jnp.concatenate([first, first, second], axis=1), jnp.concatenate([high, low, high], axis=0), preferred_element_type=F32
    )


def overlap(low_edge, high_edge, cells):
    begin = cells * CELL
    covered = jnp.minimum(high_edge, begin + CELL) - jnp.maximum(low_edge, begin)
    return jnp.maximum(covered, 0.0)


def gauss(cells, places):
    rate = math.sqrt(math.log2(math.e)) / BETA
    level = -math.log2(math.sqrt(math.pi) * BETA)
    scaled = cells * rate - places.astype(F32) * rate
    square = scaled * scaled
    return jnp.where(square <= (rate * (REACH + 0.5)) ** 2, jnp.exp2(level - square), 0.0)


def iota(shape, axis):
    return lax.broadcasted_iota(jnp.int32, shape, axis)


def is_even(axis):
    return lax.rem(lax.axis_index(axis), 2) == 0


def sides(from_even, from_odd):
    col = lax.axis_index("col")
    even = lax.rem(col, 2) == 0
    left = jnp.where(even, from_odd, from_even)
    right = jnp.where(even, from_even, from_odd)
    return jnp.where(col == 0, 0.0, left), jnp.where(col == NTC - 1, 0.0, right)


def outer_rows(from_even, from_odd):
    row = lax.axis_index("row")
    even = lax.rem(row, 2) == 0
    above = jnp.where(even, from_odd, from_even)
    below = jnp.where(even, from_even, from_odd)
    return jnp.concatenate([jnp.where(row == 0, 0.0, above), jnp.where(row == NTR - 1, 0.0, below)], axis=0)


def send_rows(edges, send_even, send_odd):
    even = is_even("row")
    top, bottom = edges[:REACH], edges[REACH:]
    send_even[...] = jnp.where(even, bottom, top)
    send_odd[...] = jnp.where(even, top, bottom)


def boxes_of(tile):
    return [tile[k].astype(jnp.int32) for k in range(4)]


def cells_from(first, count):
    return (iota((count, SLOTS), 0) + first).astype(F32)


def edge_part(py):
    return jnp.concatenate([py[:REACH, :], py[CG - REACH :, :]], axis=0).astype(F32)


def start_kernel(boxes_in, counts_in, tails_in, doses_in, tile, boxes, counts, tails, doses, arrived):
    copies = [
        pltpu.make_async_copy(source, target, arrived.at[k])
        for k, (source, target) in enumerate(((boxes_in, boxes), (counts_in, counts), (tails_in, tails), (doses_in, doses)))
    ]
    for copy in copies:
        copy.start()
    for copy in copies:
        copy.wait()
    col = lax.axis_index("col")
    totals = (counts[...] - 1) * BLK + tails[...]
    total = jnp.sum(jnp.where(iota((1, NTC), 1) == col, totals, 0), axis=1, keepdims=True)
    live = iota((1, SLOTS), 1) < total
    for k in range(4):
        tile[k] = boxes[k].astype(F32)
    tile[4] = jnp.where(live, doses[...], 0.0)


def as_columns(dose):
    return jnp.transpose(jnp.concatenate([dose[:, k * BLK : (k + 1) * BLK] for k in range(MAXB)], axis=0))


def folded_sum(value):
    return jnp.sum(value.reshape(BLK // 8, 8, SLOTS), axis=0)


def early_kernel(tile, gain_in, px_out, py_out, pairs, told, gain, gain_parts, picked, chosen_x, arrived):
    copy = pltpu.make_async_copy(gain_in, gain, arrived)
    copy.start()
    inverse = 1.0 / FORWARD_RANGE
    box = [tile[k] for k in range(4)]
    pixel_x = jnp.floor((box[0] + box[2]) * 0.5)
    pixel_y = jnp.floor((box[1] + box[3]) * 0.5)
    centre_x = jnp.broadcast_to((box[0] + box[2]) * (0.5 * inverse), (8, SLOTS))
    centre_y = jnp.broadcast_to((box[1] + box[3]) * (0.5 * inverse), (8, SLOTS))
    columns = jnp.concatenate([b * inverse for b in box] + [tile[4] * 0.25, jnp.zeros((3, SLOTS), F32)], axis=0)
    total = jnp.zeros((8, SLOTS), F32)
    dot_at = (3, 4, 5, 6)

    def find(part):
        lanes = slice(part * 256, part * 256 + 256)
        here = jnp.broadcast_to(pixel_y[:, lanes], (8, 256))
        found = jnp.zeros((8, 256), F32)
        for row in range(0, TILE, 8):
            found += jnp.where((iota((8, 256), 0) + row).astype(F32) == here, picked[part, row : row + 8, :], 0.0)
        told[1, :, lanes] = jnp.sum(found, axis=0, keepdims=True)

    for block in range(MAXB):
        at = block * BLK
        if block == dot_at[0]:
            copy.wait()
            for first in range(0, TILE, 64):
                high, low = two_parts(gain[first : first + 64, :])
                gain_parts[first : first + 64, :] = jnp.concatenate([high, low], axis=1)
        for part in range(4):
            if block == dot_at[part]:
                chosen = chosen_x[:, part * 256 : part * 256 + 256]
                picked[part] = jnp.dot(gain_parts[...], jnp.concatenate([chosen, chosen], axis=0), preferred_element_type=F32)
        side = jnp.transpose(columns[:, at : at + BLK])
        for down in range(0, BLK, 8):
            rows = slice(down, down + 8)
            low_x, low_y, high_x, high_y, dose = [side[rows, k : k + 1] for k in range(5)]
            along_x = lax.erf(centre_x - low_x) - lax.erf(centre_x - high_x)
            along_y = lax.erf(centre_y - low_y) - lax.erf(centre_y - high_y)
            values = along_x * along_y
            pairs[at + down : at + down + 8, :] = values
            total += dose * values
        if block < dot_at[0]:
            share = TILE // dot_at[0] // 16 * 16 + 16
            for first in range(block * share, min(block * share + share, TILE), 16):
                chosen_x[first : first + 16, :] = jnp.where(cells_from(first, 16) == pixel_x, 1.0, 0.0).astype(BF16)
        for part in range(4):
            if block == min(dot_at[part] + 1, MAXB - 1):
                find(part)
        if block >= dot_at[0]:
            share = 32
            begin = (block - dot_at[0]) * share
            for first in range(begin, min(begin + share, CG), 16):
                px_out[first : first + 16, :] = overlap(box[0], box[2], cells_from(first, 16)).astype(BF16)
                py_out[first : first + 16, :] = overlap(box[1], box[3], cells_from(first, 16)).astype(BF16)
    told[0] = jnp.sum(total, axis=0, keepdims=True)


def first_strips_kernel(own, got_even, got_odd, px, py, left_out, right_out, px_left, px_right, send_even, send_odd):
    left, right = sides(got_even[...], got_odd[...])
    left_out[...] = left
    right_out[...] = right
    edge_cells = jnp.concatenate([cells_from(0, REACH), cells_from(CG - REACH, REACH)], axis=0)
    edges = [stacked_dot(edge_part(py) * (own[4] * PER_CELL), px[...], NT)]
    for tile, px_out in ((left, px_left), (right, px_right)):
        across = overlap(tile[0], tile[2], cells_from(0, CG)).astype(BF16)
        px_out[...] = across
        edges.append(stacked_dot(overlap(tile[1], tile[3], edge_cells) * (tile[4] * PER_CELL), across, NT))
    send_rows(jnp.concatenate([edges[1], edges[0], edges[2]], axis=1), send_even, send_odd)


def strips(doses, px, py, send_even, send_odd):
    edges = [stacked_dot(edge_part(down) * (dose * PER_CELL), across[...], NT) for dose, across, down in zip(doses, px, py)]
    send_rows(jnp.concatenate(edges, axis=1), send_even, send_odd)


def last_strips(doses, px, py, send_even, send_odd):
    edges = [
        stacked_dot(edge_part(py[1]) * (doses[1] * PER_CELL), px[1][...], NT),
        stacked_dot(edge_part(py[0]) * (doses[0] * PER_CELL), px[0][CG - REACH :, :], NT),
        stacked_dot(edge_part(py[2]) * (doses[2] * PER_CELL), px[2][:REACH, :], NT),
        jnp.zeros((2 * REACH, 2 * CG - ALL), F32),
    ]
    send_rows(jnp.concatenate(edges, axis=1), send_even, send_odd)


def per_tile(left, own, right, margin):
    return (
        jnp.concatenate([left[CG - margin :], own[:REACH]], axis=0),
        jnp.concatenate([own, left[CG - REACH :], right[:REACH]], axis=0),
        jnp.concatenate([right[:margin], own[CG - REACH :]], axis=0),
    )


def weights_along(wx, margin):
    left, own, right = wx
    return left[CG - margin :, :], own[...], jnp.concatenate([right[:margin, :], right[CG:, :]], axis=0)


def inner_sums(doses, px, py, wy_high, wy_low, wx, inner, margin):
    coarse = [stacked_dot(across.astype(F32) * (dose * PER_CELL), down, NT) for dose, across, down in zip(doses, px, py)]
    for k, (columns, along) in enumerate(zip(per_tile(*coarse, margin), weights_along(wx, margin))):
        across = weighted(columns, wy_high[k, :CG, :], wy_low[k, :CG, :])
        inner[k] = jnp.sum(across * along, axis=0, keepdims=True)


def late_kernel(own, left, right, px_left, px, px_right, py, py_left, py_right, wy_high, wy_low, wx_left, wx, wx_right, inner):
    tiles = (left, own, right)
    boxes = [boxes_of(tile) for tile in tiles]
    cells = [[((box[k] + box[k + 2]) // (2 * CELL)).astype(F32) for k in range(2)] for box in boxes]
    for at in range(0, ALL, 16):
        apart = CG + REACH if CG <= at < CG + REACH else (REACH if at >= CG + REACH else 0)
        outer = iota((16, 1), 0) + (at - apart)
        for k, box_cells in enumerate(cells):
            wy_high[k, at : at + 16, :], wy_low[k, at : at + 16, :] = two_parts(gauss(box_cells[1], outer))
        wx[at : at + 16, :] = gauss(cells[1][0], outer)
        if at < SIDE:
            columns = iota((16, 1), 0) + at
            wx_left[at : at + 16, :] = gauss(cells[0][0], columns)
            wx_right[at : at + 16, :] = gauss(cells[2][0], columns if at < CG else columns - SIDE)
    for tile, out in ((left, py_left), (right, py_right)):
        out[...] = overlap(tile[1], tile[3], cells_from(0, CG)).astype(BF16)
    inner_sums(
        [tile[4] for tile in tiles],
        (px_left[...], px[...], px_right[...]),
        (py_left[...], py[...], py_right[...]),
        wy_high,
        wy_low,
        (wx_left, wx, wx_right),
        inner,
        MARGINS[0],
    )


def inner_kernel(doses, px_left, px, px_right, py_left, py, py_right, wy_high, wy_low, wx_left, wx, wx_right, inner):
    inner_sums(
        [doses[k] for k in range(3)],
        (px_left[...], px[...], px_right[...]),
        (py_left[...], py[...], py_right[...]),
        wy_high,
        wy_low,
        (wx_left, wx, wx_right),
        inner,
        MARGINS[1],
    )


def last_inner_kernel(doses, px_left, px, px_right, py_left, py, py_right, wy_high, wy_low, wx, pairs, inner, forward):
    coarse = jnp.concatenate(
        [
            stacked_dot(px[...].astype(F32) * (doses[1] * PER_CELL), py[...], NT),
            stacked_dot(px_left[CG - REACH :, :].astype(F32) * (doses[0] * PER_CELL), py_left[...], NT),
            stacked_dot(px_right[:REACH, :].astype(F32) * (doses[2] * PER_CELL), py_right[...], NT),
        ],
        axis=0,
    )
    across = weighted(coarse, wy_high[1, :CG, :], wy_low[1, :CG, :])
    inner[...] = jnp.sum(across * wx[...], axis=0, keepdims=True)
    forward[...] = pair_sum(doses[1], pairs)


def pair_sum(dose, pairs):
    columns = as_columns(dose * 0.25)
    total = jnp.zeros((8, SLOTS), F32)
    for k in range(MAXB):
        total += folded_sum(columns[:, k : k + 1] * pairs[k * BLK : (k + 1) * BLK, :])
    return jnp.sum(total, axis=0, keepdims=True)


def exposed(dose, sens, forward, background):
    live = dose > 0.0
    exposure = sens * (forward + BACK_RATIO * background) / (1.0 + BACK_RATIO)
    return jnp.where(live, dose * TARGET_LEVEL / jnp.where(live, exposure, 1.0), 0.0), jnp.where(live, exposure, 0.0)


def new_doses(got_even, got_odd, doses, sens, forward, inner, wy_high, wy_low, wx, margin):
    outer = outer_rows(got_even[...], got_odd[...])
    outer_t = [jnp.transpose(outer[:, k * CG : (k + 1) * CG]) for k in range(3)]
    result = []
    for k, (columns, along) in enumerate(zip(per_tile(*outer_t, margin), weights_along(wx, margin))):
        across = weighted(columns, wy_high[k, CG:, :], wy_low[k, CG:, :])
        background = inner[k] + jnp.sum(across * along, axis=0, keepdims=True)
        result.append(exposed(doses[k], sens[k], forward[k], background)[0])
    return result


def first_update_kernel(
    got_even, got_odd, told, told_even, told_odd, own, left, right, inner, pairs, px_left, px, px_right, py_left, py, py_right,
    wy_high, wy_low, wx_left, wx, wx_right, doses_out, sens_out, told_out, send_even, send_odd,
):
    told_left, told_right = sides(told_even[...], told_odd[...])
    forward, sens = zip((told_left[0], told_left[1]), (told[0], told[1]), (told_right[0], told_right[1]))
    doses = new_doses(got_even, got_odd, (left[4], own[4], right[4]), sens, forward, inner, wy_high, wy_low, (wx_left, wx, wx_right), MARGINS[0])
    for k in range(3):
        sens_out[k] = sens[k]
        doses_out[k] = doses[k]
    told_out[0] = pair_sum(doses[1], pairs)
    strips(doses, (px_left, px, px_right), (py_left, py, py_right), send_even, send_odd)


def update_kernel(
    got_even, got_odd, told, told_even, told_odd, doses, sens, inner, px_left, px, px_right, py_left, py, py_right,
    wy_high, wy_low, wx_left, wx, wx_right, doses_out, send_even, send_odd,
):
    told_left, told_right = sides(told_even[...], told_odd[...])
    before = [doses[k] for k in range(3)]
    factors = [sens[k] for k in range(3)]
    forward = (told_left[0], told[0], told_right[0])
    after = new_doses(got_even, got_odd, before, factors, forward, inner, wy_high, wy_low, (wx_left, wx, wx_right), MARGINS[1])
    for k in range(3):
        doses_out[k] = after[k]
    last_strips(after, (px_left, px, px_right), (py_left, py, py_right), send_even, send_odd)


def last_result(got_even, got_odd, doses, sens, inner, forward, wy_high, wy_low, wx, results):
    dose_out, exposure_out, dose, exposure, sent = results
    outer = outer_rows(got_even[...], got_odd[...])
    columns = jnp.concatenate([jnp.transpose(outer[:, :CG]), jnp.transpose(outer[:, CG:])[: 2 * REACH]], axis=0)
    across = weighted(columns, wy_high[1, CG:, :], wy_low[1, CG:, :])
    background = inner[...] + jnp.sum(across * wx[...], axis=0, keepdims=True)
    dose[...], exposure[...] = exposed(doses[1], sens[1], forward[...], background)
    copies = [pltpu.make_async_copy(dose, dose_out, sent.at[0]), pltpu.make_async_copy(exposure, exposure_out, sent.at[1])]
    for copy in copies:
        copy.start()
    for copy in copies:
        copy.wait()


def at_window_edge():
    row = lax.axis_index("row")
    return (row == 0) | (row == NTR - 1)


def edge_kernel(got_even, doses, sens, inner, forward, wy_high, wy_low, wx, *results):
    @pl.when(at_window_edge())
    def _():
        last_result(got_even, got_even, doses, sens, inner, forward, wy_high, wy_low, wx, results)


def final_kernel(got_even, got_odd, doses, sens, inner, forward, wy_high, wy_low, wx, edge_dose, edge_exposure, *results):
    @pl.when(jnp.logical_not(at_window_edge()))
    def _():
        last_result(got_even, got_odd, doses, sens, inner, forward, wy_high, wy_low, wx, results)


def shape(*dims, dtype=F32):
    return jax.ShapeDtypeStruct(dims, dtype)


HBM = pl.BlockSpec(memory_space=pltpu.HBM)
VMEM = pl.BlockSpec(memory_space=pltpu.VMEM)


def call(kernel, outs, vmem=24, ins=None, scratch=(), **extra):
    if ins is not None:
        extra["in_specs"] = ins
    return pl.pallas_call(
        kernel,
        out_shape=outs,
        scratch_shapes=scratch,
        compiler_params=pltpu.CompilerParams(vmem_limit_bytes=vmem << 20),
        **extra,
    )


def in_hbm(*arrays):
    return [pltpu.with_memory_space_constraint(array, pltpu.HBM) for array in arrays]


def send(value, table):
    return lax.ppermute(value, AXES, table)


def body(shot_boxes, block_counts, tail_shots, doses, pixel_gain):
    row_even, row_odd, col_even, col_odd = pairings()
    row = shape(1, SLOTS)
    rows = shape(3, 1, SLOTS)
    cover = shape(CG, SLOTS, dtype=BF16)
    tile = shape(5, 1, SLOTS)
    weights = shape(3, ALL, SLOTS, dtype=BF16)
    strip = shape(REACH, 3 * CG)
    short = shape(REACH, 2 * CG)
    own = call(
        start_kernel,
        tile,
        ins=[HBM] * 4,
        scratch=(
            pltpu.VMEM((4, 1, SLOTS), jnp.int32),
            pltpu.VMEM((1, NTC), jnp.int32),
            pltpu.VMEM((1, NTC), jnp.int32),
            pltpu.VMEM((1, SLOTS), F32),
            pltpu.SemaphoreType.DMA((4,)),
        ),
    )(*in_hbm(shot_boxes, block_counts, tail_shots, doses))
    far_odd = send(own, col_odd)
    far_even = send(own, col_even)
    px, py, pairs, told = call(
        early_kernel,
        (cover, cover, shape(SLOTS, SLOTS), shape(2, 1, SLOTS)),
        ins=[VMEM, HBM],
        scratch=(
            pltpu.VMEM((TILE, TILE), F32),
            pltpu.VMEM((TILE, 2 * TILE), BF16),
            pltpu.VMEM((4, TILE, 256), F32),
            pltpu.VMEM((TILE, SLOTS), BF16),
            pltpu.SemaphoreType.DMA,
        ),
    )(own, *in_hbm(pixel_gain))
    told_odd = send(told, col_odd)
    left, right, px_left, px_right, strip_even, strip_odd = call(
        first_strips_kernel, (tile, tile, cover, cover, strip, strip)
    )(own, far_even, far_odd, px, py)
    got_odd = send(strip_odd, row_odd)
    got_even = send(strip_even, row_even)
    told_even = send(told, col_even)
    py_left, py_right, wy_high, wy_low, wx_left, wx, wx_right, inner = call(
        late_kernel, (cover, cover, weights, weights, shape(SIDE, SLOTS), shape(ALL, SLOTS), shape(SIDE, SLOTS), rows)
    )(own, left, right, px_left, px, px_right, py)
    covers = (px_left, px, px_right, py_left, py, py_right)
    weighing = (wy_high, wy_low, wx_left, wx, wx_right)
    doses3, sens, told_next, strip_even, strip_odd = call(first_update_kernel, (rows, rows, shape(1, 1, SLOTS), strip, strip))(
        got_even, got_odd, told, told_even, told_odd, own, left, right, inner, pairs, *covers, *weighing
    )
    told_odd = send(told_next, col_odd)
    got_odd = send(strip_odd, row_odd)
    told_even = send(told_next, col_even)
    got_even = send(strip_even, row_even)
    inner = call(inner_kernel, rows)(doses3, *covers, *weighing)
    doses3, strip_even, strip_odd = call(update_kernel, (rows, short, short))(
        got_even, got_odd, told_next, told_even, told_odd, doses3, sens, inner, *covers, *weighing
    )
    got_odd = send(strip_odd, row_odd)
    got_even = send(strip_even, row_even)
    inner, forward = call(last_inner_kernel, (row, row))(doses3, *covers, wy_high, wy_low, wx, pairs)
    results = {
        "out_specs": (HBM, HBM),
        "scratch": (pltpu.VMEM((1, SLOTS), F32), pltpu.VMEM((1, SLOTS), F32), pltpu.SemaphoreType.DMA((2,))),
    }
    common = (doses3, sens, inner, forward, wy_high, wy_low, wx)
    edge = call(edge_kernel, (row, row), **results)(got_even, *common)
    return call(final_kernel, (row, row), ins=[VMEM] * 9 + [HBM] * 2, input_output_aliases={9: 0, 10: 1}, **results)(
        got_even, got_odd, *common, *edge
    )


def solution(mesh):
    placed = (P(None, "row", "col"), P("row", None), P("row", None), P("row", "col"), P("row", "col"))
    return jax.shard_map(body, mesh=mesh, in_specs=placed, out_specs=(P("row", "col"), P("row", "col")), check_vma=False)
```

```python
import math

import jax
import jax.numpy as jnp
from jax import lax
from jax.experimental import pallas as pl
from jax.experimental.pallas import tpu as pltpu
from jax.sharding import PartitionSpec as P


TILE = 512
CG = 128
BLK = 128
CELL = 4
BETA = 16
REACH = 32
SLOTS = 1024
NTR = 8
NTC = 16
FORWARD_RANGE = 4.0
BACK_RATIO = 0.75
TARGET_LEVEL = 1.0
F32 = jnp.float32
BF16 = jnp.bfloat16
AXES = ("row", "col")
NT = (((1,), (1,)), ((), ()))
MAXB = 8
SIDE = CG + REACH
PER_CELL = 1.0 / CELL**2
ALL = CG + 2 * REACH
MARGINS = (3 * REACH + 2 * 8, 2 * REACH + 8)


def pairings():
    def number(r, c):
        return r * NTC + c

    def table(partner):
        return [(number(r, c), number(*partner(r, c))) for r in range(NTR) for c in range(NTC)]

    def odd(i):
        return ((i - 1) ^ 1) + 1

    row_even = table(lambda r, c: (r ^ 1, c))
    row_odd = table(lambda r, c: (r, c ^ 1) if r in (0, NTR - 1) else (odd(r), c))
    col_even = table(lambda r, c: (r, c ^ 1))
    col_odd = table(lambda r, c: (r ^ 1, c) if c in (0, NTC - 1) else (r, odd(c)))
    return row_even, row_odd, col_even, col_odd


def two_parts(value):
    high = value.astype(BF16)
    low = (value - high.astype(F32)).astype(BF16)
    return high, low


def stacked_dot(value, other, dims):
    rows = value.shape[0]
    parts = jnp.concatenate(two_parts(value), axis=0)
    both = lax.dot_general(parts, other, dims, preferred_element_type=F32)
    return both[:rows] + both[rows:]


def weighted(columns, high, low):
    first, second = two_parts(columns)
    return jnp.dot(
        jnp.concatenate([first, first, second], axis=1), jnp.concatenate([high, low, high], axis=0), preferred_element_type=F32
    )


def overlap(low_edge, high_edge, cells):
    begin = cells * CELL
    covered = jnp.minimum(high_edge, begin + CELL) - jnp.maximum(low_edge, begin)
    return jnp.maximum(covered, 0.0)


def gauss(cells, places):
    rate = math.sqrt(math.log2(math.e)) / BETA
    level = -math.log2(math.sqrt(math.pi) * BETA)
    scaled = cells * rate - places.astype(F32) * rate
    square = scaled * scaled
    return jnp.where(square <= (rate * (REACH + 0.5)) ** 2, jnp.exp2(level - square), 0.0)


def iota(shape, axis):
    return lax.broadcasted_iota(jnp.int32, shape, axis)


def is_even(axis):
    return lax.rem(lax.axis_index(axis), 2) == 0


def sides(from_even, from_odd):
    col = lax.axis_index("col")
    even = lax.rem(col, 2) == 0
    left = jnp.where(even, from_odd, from_even)
    right = jnp.where(even, from_even, from_odd)
    return jnp.where(col == 0, 0.0, left), jnp.where(col == NTC - 1, 0.0, right)


def outer_rows(from_even, from_odd):
    row = lax.axis_index("row")
    even = lax.rem(row, 2) == 0
    above = jnp.where(even, from_odd, from_even)
    below = jnp.where(even, from_even, from_odd)
    return jnp.concatenate([jnp.where(row == 0, 0.0, above), jnp.where(row == NTR - 1, 0.0, below)], axis=0)


def send_rows(edges, send_even, send_odd):
    even = is_even("row")
    top, bottom = edges[:REACH], edges[REACH:]
    send_even[...] = jnp.where(even, bottom, top)
    send_odd[...] = jnp.where(even, top, bottom)


def boxes_of(tile):
    return [tile[k].astype(jnp.int32) for k in range(4)]


def cells_from(first, count):
    return (iota((count, SLOTS), 0) + first).astype(F32)


def edge_part(py):
    return jnp.concatenate([py[:REACH, :], py[CG - REACH :, :]], axis=0).astype(F32)


def start_kernel(boxes_in, counts_in, tails_in, doses_in, tile, boxes, counts, tails, doses, arrived):
    copies = [
        pltpu.make_async_copy(source, target, arrived.at[k])
        for k, (source, target) in enumerate(((boxes_in, boxes), (counts_in, counts), (tails_in, tails), (doses_in, doses)))
    ]
    for copy in copies:
        copy.start()
    for copy in copies:
        copy.wait()
    col = lax.axis_index("col")
    totals = (counts[...] - 1) * BLK + tails[...]
    total = jnp.sum(jnp.where(iota((1, NTC), 1) == col, totals, 0), axis=1, keepdims=True)
    live = iota((1, SLOTS), 1) < total
    for k in range(4):
        tile[k] = boxes[k].astype(F32)
    tile[4] = jnp.where(live, doses[...], 0.0)


def as_columns(dose):
    return jnp.transpose(jnp.concatenate([dose[:, k * BLK : (k + 1) * BLK] for k in range(MAXB)], axis=0))


def folded_sum(value):
    return jnp.sum(value.reshape(BLK // 8, 8, SLOTS), axis=0)


def early_kernel(tile, gain_in, px_out, py_out, pairs, told, gain, gain_parts, picked, chosen_x, arrived):
    copy = pltpu.make_async_copy(gain_in, gain, arrived)
    copy.start()
    inverse = 1.0 / FORWARD_RANGE
    box = [tile[k] for k in range(4)]
    pixel_x = jnp.floor((box[0] + box[2]) * 0.5)
    pixel_y = jnp.floor((box[1] + box[3]) * 0.5)
    centre_x = jnp.broadcast_to((box[0] + box[2]) * (0.5 * inverse), (8, SLOTS))
    centre_y = jnp.broadcast_to((box[1] + box[3]) * (0.5 * inverse), (8, SLOTS))
    columns = jnp.concatenate([b * inverse for b in box] + [tile[4] * 0.25, jnp.zeros((3, SLOTS), F32)], axis=0)
    total = jnp.zeros((8, SLOTS), F32)
    dot_at = (4, 5, 6, 7)

    def find(part):
        lanes = slice(part * 256, part * 256 + 256)
        here = jnp.broadcast_to(pixel_y[:, lanes], (8, 256))
        found = jnp.zeros((8, 256), F32)
        for row in range(0, TILE, 8):
            found += jnp.where((iota((8, 256), 0) + row).astype(F32) == here, picked[part, row : row + 8, :], 0.0)
        told[1, :, lanes] = jnp.sum(found, axis=0, keepdims=True)

    for block in range(MAXB):
        at = block * BLK
        if block == dot_at[0]:
            copy.wait()
            for first in range(0, TILE, 64):
                high, low = two_parts(gain[first : first + 64, :])
                gain_parts[first : first + 64, :] = jnp.concatenate([high, low], axis=1)
        for part in range(4):
            if block == dot_at[part]:
                chosen = chosen_x[:, part * 256 : part * 256 + 256]
                picked[part] = jnp.dot(gain_parts[...], jnp.concatenate([chosen, chosen], axis=0), preferred_element_type=F32)
        side = jnp.transpose(columns[:, at : at + BLK])
        for down in range(0, BLK, 8):
            rows = slice(down, down + 8)
            low_x, low_y, high_x, high_y, dose = [side[rows, k : k + 1] for k in range(5)]
            along_x = lax.erf(centre_x - low_x) - lax.erf(centre_x - high_x)
            along_y = lax.erf(centre_y - low_y) - lax.erf(centre_y - high_y)
            values = along_x * along_y
            pairs[at + down : at + down + 8, :] = values
            total += dose * values
        if block < dot_at[0]:
            share = TILE // dot_at[0] // 16 * 16 + 16
            for first in range(block * share, min(block * share + share, TILE), 16):
                chosen_x[first : first + 16, :] = jnp.where(cells_from(first, 16) == pixel_x, 1.0, 0.0).astype(BF16)
        for part in range(4):
            if block == min(dot_at[part] + 1, MAXB - 1):
                find(part)
        if block >= dot_at[0]:
            share = 32
            begin = (block - dot_at[0]) * share
            for first in range(begin, min(begin + share, CG), 16):
                px_out[first : first + 16, :] = overlap(box[0], box[2], cells_from(first, 16)).astype(BF16)
                py_out[first : first + 16, :] = overlap(box[1], box[3], cells_from(first, 16)).astype(BF16)
    told[0] = jnp.sum(total, axis=0, keepdims=True)


def first_strips_kernel(own, got_even, got_odd, px, py, left_out, right_out, px_left, px_right, send_even, send_odd):
    left, right = sides(got_even[...], got_odd[...])
    left_out[...] = left
    right_out[...] = right
    edge_cells = jnp.concatenate([cells_from(0, REACH), cells_from(CG - REACH, REACH)], axis=0)
    edges = [stacked_dot(edge_part(py) * (own[4] * PER_CELL), px[...], NT)]
    for tile, px_out in ((left, px_left), (right, px_right)):
        across = overlap(tile[0], tile[2], cells_from(0, CG)).astype(BF16)
        px_out[...] = across
        edges.append(stacked_dot(overlap(tile[1], tile[3], edge_cells) * (tile[4] * PER_CELL), across, NT))
    send_rows(jnp.concatenate([edges[1], edges[0], edges[2]], axis=1), send_even, send_odd)


def strips(doses, px, py, send_even, send_odd):
    edges = [stacked_dot(edge_part(down) * (dose * PER_CELL), across[...], NT) for dose, across, down in zip(doses, px, py)]
    send_rows(jnp.concatenate(edges, axis=1), send_even, send_odd)


def last_strips(doses, px, py, send_even, send_odd):
    edges = [
        stacked_dot(edge_part(py[1]) * (doses[1] * PER_CELL), px[1][...], NT),
        stacked_dot(edge_part(py[0]) * (doses[0] * PER_CELL), px[0][CG - REACH :, :], NT),
        stacked_dot(edge_part(py[2]) * (doses[2] * PER_CELL), px[2][:REACH, :], NT),
    ]
    beside = jnp.concatenate(edges[1:], axis=1)
    half = REACH // 2
    folded = [
        jnp.concatenate([edges[0][at : at + REACH], jnp.concatenate([beside[at : at + half], beside[at + half : at + REACH]], axis=1)], axis=0)
        for at in (0, REACH)
    ]
    even = is_even("row")
    send_even[...] = jnp.where(even, folded[1], folded[0])
    send_odd[...] = jnp.where(even, folded[0], folded[1])


def per_tile(left, own, right, margin):
    return (
        jnp.concatenate([left[CG - margin :], own[:REACH]], axis=0),
        jnp.concatenate([own, left[CG - REACH :], right[:REACH]], axis=0),
        jnp.concatenate([right[:margin], own[CG - REACH :]], axis=0),
    )


def weights_along(wx, margin):
    left, own, right = wx
    return left[CG - margin :, :], own[...], jnp.concatenate([right[:margin, :], right[CG:, :]], axis=0)


def inner_sums(doses, px, py, wy_high, wy_low, wx, inner, margin):
    coarse = [stacked_dot(across.astype(F32) * (dose * PER_CELL), down, NT) for dose, across, down in zip(doses, px, py)]
    for k, (columns, along) in enumerate(zip(per_tile(*coarse, margin), weights_along(wx, margin))):
        across = weighted(columns, wy_high[k, :CG, :], wy_low[k, :CG, :])
        inner[k] = jnp.sum(across * along, axis=0, keepdims=True)


def late_kernel(own, left, right, px_left, px, px_right, py, py_left, py_right, wy_high, wy_low, wx_left, wx, wx_right, inner):
    tiles = (left, own, right)
    boxes = [boxes_of(tile) for tile in tiles]
    cells = [[((box[k] + box[k + 2]) // (2 * CELL)).astype(F32) for k in range(2)] for box in boxes]
    for at in range(0, ALL, 16):
        apart = CG + REACH if CG <= at < CG + REACH else (REACH if at >= CG + REACH else 0)
        outer = iota((16, 1), 0) + (at - apart)
        for k, box_cells in enumerate(cells):
            wy_high[k, at : at + 16, :], wy_low[k, at : at + 16, :] = two_parts(gauss(box_cells[1], outer))
        wx[at : at + 16, :] = gauss(cells[1][0], outer)
        if at < SIDE:
            columns = iota((16, 1), 0) + at
            wx_left[at : at + 16, :] = gauss(cells[0][0], columns)
            wx_right[at : at + 16, :] = gauss(cells[2][0], columns if at < CG else columns - SIDE)
    for tile, out in ((left, py_left), (right, py_right)):
        out[...] = overlap(tile[1], tile[3], cells_from(0, CG)).astype(BF16)
    inner_sums(
        [tile[4] for tile in tiles],
        (px_left[...], px[...], px_right[...]),
        (py_left[...], py[...], py_right[...]),
        wy_high,
        wy_low,
        (wx_left, wx, wx_right),
        inner,
        MARGINS[0],
    )


def inner_kernel(doses, px_left, px, px_right, py_left, py, py_right, wy_high, wy_low, wx_left, wx, wx_right, inner):
    inner_sums(
        [doses[k] for k in range(3)],
        (px_left[...], px[...], px_right[...]),
        (py_left[...], py[...], py_right[...]),
        wy_high,
        wy_low,
        (wx_left, wx, wx_right),
        inner,
        MARGINS[1],
    )


def last_inner_kernel(doses, px_left, px, px_right, py_left, py, py_right, wy_high, wy_low, wx, pairs, inner, forward):
    coarse = jnp.concatenate(
        [
            stacked_dot(px[...].astype(F32) * (doses[1] * PER_CELL), py[...], NT),
            stacked_dot(px_left[CG - REACH :, :].astype(F32) * (doses[0] * PER_CELL), py_left[...], NT),
            stacked_dot(px_right[:REACH, :].astype(F32) * (doses[2] * PER_CELL), py_right[...], NT),
        ],
        axis=0,
    )
    across = weighted(coarse, wy_high[1, :CG, :], wy_low[1, :CG, :])
    inner[...] = jnp.sum(across * wx[...], axis=0, keepdims=True)
    forward[...] = pair_sum(doses[1], pairs)


def pair_sum(dose, pairs):
    columns = as_columns(dose * 0.25)
    total = jnp.zeros((8, SLOTS), F32)
    for k in range(MAXB):
        total += folded_sum(columns[:, k : k + 1] * pairs[k * BLK : (k + 1) * BLK, :])
    return jnp.sum(total, axis=0, keepdims=True)


def exposed(dose, sens, forward, background):
    live = dose > 0.0
    exposure = sens * (forward + BACK_RATIO * background) / (1.0 + BACK_RATIO)
    return jnp.where(live, dose * TARGET_LEVEL / jnp.where(live, exposure, 1.0), 0.0), jnp.where(live, exposure, 0.0)


def new_doses(got_even, got_odd, doses, sens, forward, inner, wy_high, wy_low, wx, margin):
    outer = outer_rows(got_even[...], got_odd[...])
    outer_t = [jnp.transpose(outer[:, k * CG : (k + 1) * CG]) for k in range(3)]
    result = []
    for k, (columns, along) in enumerate(zip(per_tile(*outer_t, margin), weights_along(wx, margin))):
        across = weighted(columns, wy_high[k, CG:, :], wy_low[k, CG:, :])
        background = inner[k] + jnp.sum(across * along, axis=0, keepdims=True)
        result.append(exposed(doses[k], sens[k], forward[k], background)[0])
    return result


def first_update_kernel(
    got_even, got_odd, told, told_even, told_odd, own, left, right, inner, pairs, px_left, px, px_right, py_left, py, py_right,
    wy_high, wy_low, wx_left, wx, wx_right, doses_out, sens_out, told_out, send_even, send_odd,
):
    told_left, told_right = sides(told_even[...], told_odd[...])
    forward, sens = zip((told_left[0], told_left[1]), (told[0], told[1]), (told_right[0], told_right[1]))
    doses = new_doses(got_even, got_odd, (left[4], own[4], right[4]), sens, forward, inner, wy_high, wy_low, (wx_left, wx, wx_right), MARGINS[0])
    for k in range(3):
        sens_out[k] = sens[k]
        doses_out[k] = doses[k]
    told_out[0] = pair_sum(doses[1], pairs)
    strips(doses, (px_left, px, px_right), (py_left, py, py_right), send_even, send_odd)


def update_kernel(
    got_even, got_odd, told, told_even, told_odd, doses, sens, inner, px_left, px, px_right, py_left, py, py_right,
    wy_high, wy_low, wx_left, wx, wx_right, doses_out, send_even, send_odd,
):
    told_left, told_right = sides(told_even[...], told_odd[...])
    before = [doses[k] for k in range(3)]
    factors = [sens[k] for k in range(3)]
    forward = (told_left[0], told[0], told_right[0])
    after = new_doses(got_even, got_odd, before, factors, forward, inner, wy_high, wy_low, (wx_left, wx, wx_right), MARGINS[1])
    for k in range(3):
        doses_out[k] = after[k]
    last_strips(after, (px_left, px, px_right), (py_left, py, py_right), send_even, send_odd)


def last_result(got_even, got_odd, doses, sens, inner, forward, wy_high, wy_low, wx, results):
    dose_out, exposure_out, dose, exposure, sent = results
    outer = outer_rows(got_even[...], got_odd[...])
    each = REACH + REACH // 2
    middle = jnp.concatenate([outer[:REACH], outer[each : each + REACH]], axis=0)
    ends = [outer[at + REACH : at + each, side : side + 2 * REACH] for at in (0, each) for side in (0, 2 * REACH)]
    columns = jnp.concatenate([jnp.transpose(middle), jnp.transpose(jnp.concatenate(ends, axis=0))], axis=0)
    across = weighted(columns, wy_high[1, CG:, :], wy_low[1, CG:, :])
    background = inner[...] + jnp.sum(across * wx[...], axis=0, keepdims=True)
    dose[...], exposure[...] = exposed(doses[1], sens[1], forward[...], background)
    copies = [pltpu.make_async_copy(dose, dose_out, sent.at[0]), pltpu.make_async_copy(exposure, exposure_out, sent.at[1])]
    for copy in copies:
        copy.start()
    for copy in copies:
        copy.wait()


def at_window_edge():
    row = lax.axis_index("row")
    return (row == 0) | (row == NTR - 1)


def edge_kernel(got_even, doses, sens, inner, forward, wy_high, wy_low, wx, *results):
    @pl.when(at_window_edge())
    def _():
        last_result(got_even, got_even, doses, sens, inner, forward, wy_high, wy_low, wx, results)


def final_kernel(got_even, got_odd, doses, sens, inner, forward, wy_high, wy_low, wx, edge_dose, edge_exposure, *results):
    @pl.when(jnp.logical_not(at_window_edge()))
    def _():
        last_result(got_even, got_odd, doses, sens, inner, forward, wy_high, wy_low, wx, results)


def shape(*dims, dtype=F32):
    return jax.ShapeDtypeStruct(dims, dtype)


HBM = pl.BlockSpec(memory_space=pltpu.HBM)
VMEM = pl.BlockSpec(memory_space=pltpu.VMEM)


def call(kernel, outs, vmem=24, ins=None, scratch=(), **extra):
    if ins is not None:
        extra["in_specs"] = ins
    return pl.pallas_call(
        kernel,
        out_shape=outs,
        scratch_shapes=scratch,
        compiler_params=pltpu.CompilerParams(vmem_limit_bytes=vmem << 20),
        **extra,
    )


def in_hbm(*arrays):
    return [pltpu.with_memory_space_constraint(array, pltpu.HBM) for array in arrays]


def send(value, table):
    return lax.ppermute(value, AXES, table)


def body(shot_boxes, block_counts, tail_shots, doses, pixel_gain):
    row_even, row_odd, col_even, col_odd = pairings()
    row = shape(1, SLOTS)
    rows = shape(3, 1, SLOTS)
    cover = shape(CG, SLOTS, dtype=BF16)
    tile = shape(5, 1, SLOTS)
    weights = shape(3, ALL, SLOTS, dtype=BF16)
    strip = shape(REACH, 3 * CG)
    short = shape(REACH + REACH // 2, CG)
    own = call(
        start_kernel,
        tile,
        ins=[HBM] * 4,
        scratch=(
            pltpu.VMEM((4, 1, SLOTS), jnp.int32),
            pltpu.VMEM((1, NTC), jnp.int32),
            pltpu.VMEM((1, NTC), jnp.int32),
            pltpu.VMEM((1, SLOTS), F32),
            pltpu.SemaphoreType.DMA((4,)),
        ),
    )(*in_hbm(shot_boxes, block_counts, tail_shots, doses))
    far_odd = send(own, col_odd)
    far_even = send(own, col_even)
    px, py, pairs, told = call(
        early_kernel,
        (cover, cover, shape(SLOTS, SLOTS), shape(2, 1, SLOTS)),
        ins=[VMEM, HBM],
        scratch=(
            pltpu.VMEM((TILE, TILE), F32),
            pltpu.VMEM((TILE, 2 * TILE), BF16),
            pltpu.VMEM((4, TILE, 256), F32),
            pltpu.VMEM((TILE, SLOTS), BF16),
            pltpu.SemaphoreType.DMA,
        ),
    )(own, *in_hbm(pixel_gain))
    told_odd = send(told, col_odd)
    left, right, px_left, px_right, strip_even, strip_odd = call(
        first_strips_kernel, (tile, tile, cover, cover, strip, strip)
    )(own, far_even, far_odd, px, py)
    got_odd = send(strip_odd, row_odd)
    got_even = send(strip_even, row_even)
    told_even = send(told, col_even)
    py_left, py_right, wy_high, wy_low, wx_left, wx, wx_right, inner = call(
        late_kernel, (cover, cover, weights, weights, shape(SIDE, SLOTS), shape(ALL, SLOTS), shape(SIDE, SLOTS), rows)
    )(own, left, right, px_left, px, px_right, py)
    covers = (px_left, px, px_right, py_left, py, py_right)
    weighing = (wy_high, wy_low, wx_left, wx, wx_right)
    doses3, sens, told_next, strip_even, strip_odd = call(first_update_kernel, (rows, rows, shape(1, 1, SLOTS), strip, strip))(
        got_even, got_odd, told, told_even, told_odd, own, left, right, inner, pairs, *covers, *weighing
    )
    told_odd = send(told_next, col_odd)
    got_odd = send(strip_odd, row_odd)
    told_even = send(told_next, col_even)
    got_even = send(strip_even, row_even)
    inner = call(inner_kernel, rows)(doses3, *covers, *weighing)
    doses3, strip_even, strip_odd = call(update_kernel, (rows, short, short))(
        got_even, got_odd, told_next, told_even, told_odd, doses3, sens, inner, *covers, *weighing
    )
    got_odd = send(strip_odd, row_odd)
    got_even = send(strip_even, row_even)
    inner, forward = call(last_inner_kernel, (row, row))(doses3, *covers, wy_high, wy_low, wx, pairs)
    results = {
        "out_specs": (HBM, HBM),
        "scratch": (pltpu.VMEM((1, SLOTS), F32), pltpu.VMEM((1, SLOTS), F32), pltpu.SemaphoreType.DMA((2,))),
    }
    common = (doses3, sens, inner, forward, wy_high, wy_low, wx)
    edge = call(edge_kernel, (row, row), **results)(got_even, *common)
    return call(final_kernel, (row, row), ins=[VMEM] * 9 + [HBM] * 2, input_output_aliases={9: 0, 10: 1}, **results)(
        got_even, got_odd, *common, *edge
    )


def solution(mesh):
    placed = (P(None, "row", "col"), P("row", None), P("row", None), P("row", "col"), P("row", "col"))
    return jax.shard_map(body, mesh=mesh, in_specs=placed, out_specs=(P("row", "col"), P("row", "col")), check_vma=False)
```
